512 devices in a mesh: dp: 16 (over z, core), ctx: 32 (over x, y).
Axes of the slice: x: 4, y: 8, z: 8, core: 2. Of those that a mesh axis runs over, the one named last changes fastest.
Arguments:
- streams: bfloat16 [3, 1, 10240, 8192], P(None, None, 'ctx', 'dp'), may hold values from -6 to 6
- cotangent: bfloat16 [1, 10240, 8192], P(None, 'ctx', 'dp'), may hold values from -6 to 6
- counts: int32 [1, 32], P(None, 'ctx'), may hold values from 1 to 320, as said below
- short_filters: bfloat16 [3, 7, 8192], P(None, None, ('dp', 'ctx')), may hold values from -14 to 14
- long_filter: bfloat16 [128, 8192], P(None, ('dp', 'ctx')), may hold values from -0.5 to 0.5
Outputs:
- stream_grads: bfloat16 [3, 1, 10240, 8192], P(None, None, 'ctx', 'dp')
- long_grad: float32 [128, 8192], P(None, ('dp', 'ctx'))
- short_grad: float32 [3, 7, 8192], P(None, None, ('dp', 'ctx'))
The draws below stay inside these ranges and needn't reach their ends.
Inputs may be any that keep to these rules, and one draw needn't show every extreme that they name: In each window the counts sum to 8192, and one of them equals 320.
All inputs are finite; a program needn't handle non-finite values.
Results may differ from the reference program's by a relative error of at most 0.0058.
Values may be sent and summed in bfloat16 or wider, within the bound.
No kernel may reach another device: no remote copies, remote signals or barrier semaphores. Data moves between devices by JAX's collectives and lax.ppermute only.
A program may use at most 64 MiB of HBM per device.

```python
import math
import jax
import jax.numpy as jnp
from jax import lax

CH = 8192
LTAP = 128
STAP = 7
SEQS = 1
CAP = 320
SEQ_LEN = 8192
ROWS = 10240
N_CTX = 32


def draw_short_filters(key, part):
    ramp = jnp.exp(math.log(3.0) * jnp.arange(CH, dtype=jnp.float32) / float(CH))
    base = jnp.clip(jax.random.normal(key, (3, STAP, CH), jnp.float32), -4.0, 4.0)
    return (base * ramp[None, None, :] / math.sqrt(STAP)).astype(jnp.bfloat16)


def drifting_level(key, shape_lead):
    keys = jax.random.split(jax.random.fold_in(key, 71), 3)
    level = jax.random.uniform(keys[0], shape_lead + (1, CH), jnp.float32, 0.3, 0.6)
    waves = jax.random.randint(keys[1], shape_lead + (1, CH), 1, 4).astype(jnp.float32)
    phase = jax.random.uniform(keys[2], shape_lead + (1, CH), jnp.float32, -math.pi, math.pi)
    position = jnp.arange(ROWS, dtype=jnp.float32) / float(ROWS)
    position = position.reshape((1,) * len(shape_lead) + (ROWS, 1))
    return level * (1.0 + 0.5 * jnp.sin(2.0 * math.pi * waves * position + phase))


def rough_part(key, shape):
    noise_key = jax.random.fold_in(key, 73)
    return jnp.clip(jax.random.normal(noise_key, shape, jnp.float32), -4.0, 4.0)


def draw_streams(key, part):
    shape = (3, SEQS, ROWS, CH)
    values = rough_part(key, shape) + drifting_level(key, (3, SEQS))
    return values.astype(jnp.bfloat16)


def draw_cotangent(key, part):
    shape = (SEQS, ROWS, CH)
    values = rough_part(key, shape) + drifting_level(key, (SEQS,))
    return values.astype(jnp.bfloat16)


def count_row(key, run):
    keys = jax.random.split(key, 6)
    others = N_CTX - run
    spread = others - 1
    half = spread // 2
    start = jax.random.randint(keys[0], (), 1, N_CTX - run).astype(jnp.int32)
    tiny = jax.random.randint(keys[1], (run,), 1, 3).astype(jnp.int32)
    tiny = tiny.at[0].set(1)
    rest = SEQ_LEN - CAP - jnp.sum(tiny)
    base = rest // spread
    extra = rest - base * spread
    order_a = jax.random.permutation(keys[2], spread).astype(jnp.int32)
    values = base + (order_a < extra).astype(jnp.int32)
    limit = jnp.maximum(jnp.minimum(CAP - base - 1, base - 1), 0)
    moves = jax.random.randint(keys[3], (half,), 0, limit + 1).astype(jnp.int32)
    delta = jnp.concatenate([moves, jnp.zeros((spread - 2 * half,), jnp.int32), -moves[::-1]])
    order_b = jax.random.permutation(keys[4], spread).astype(jnp.int32)
    values = values + delta[order_b]
    full_at = jax.random.randint(keys[5], (), 0, others).astype(jnp.int32)
    slot = jnp.arange(others, dtype=jnp.int32)
    pick = jnp.clip(slot - (slot > full_at).astype(jnp.int32), 0, spread - 1)
    other_values = jnp.where(slot == full_at, CAP, values[pick])
    device_ids = jnp.arange(N_CTX, dtype=jnp.int32)
    in_run = (device_ids >= start) & (device_ids < start + run)
    run_index = jnp.clip(device_ids - start, 0, run - 1)
    other_index = jnp.clip(jnp.where(device_ids < start, device_ids, device_ids - run), 0, others - 1)
    return jnp.where(in_run, tiny[run_index], other_values[other_index]).astype(jnp.int32)


def draw_counts(key, part):
    run = max(1, N_CTX // 8)
    windows = []
    for window_index in range(SEQS):
        windows.append(count_row(jax.random.fold_in(key, 11 + window_index), run))
    return jnp.stack(windows).astype(jnp.int32)


def block_scale(rng, dims, shards, smallest, largest):
    def one(dim, blocks):
        heights = jax.random.uniform(jax.random.fold_in(jax.random.fold_in(rng, 6), dim), (blocks,), jnp.float32, smallest / len(shards), largest / len(shards))
        return jnp.repeat(jnp.exp(heights), dims[dim] // blocks).reshape((-1,) + (1,) * (len(dims) - dim - 1))

    level = one(*shards[0])
    for cut in shards[1:]:
        level = level * one(*cut)
    return level


def centred(stream_key, shape, width, bound, pieces=(), kind=jnp.bfloat16):
    entries = width * jax.random.normal(stream_key, shape, jnp.float32)
    if pieces:
        entries = entries * block_scale(stream_key, shape, pieces, -0.22, 0.18)
    return jnp.clip(entries, -bound, bound).astype(kind)


def setup_inputs(seed: int = 0) -> dict:
    key_list = jax.random.split(jax.random.key(seed), 6)
    streams = draw_streams(jax.random.fold_in(key_list[5], 71), 0)
    cotangent = draw_cotangent(jax.random.fold_in(key_list[5], 71), 0)
    counts = draw_counts(jax.random.fold_in(key_list[5], 71), 0)
    short_filters = draw_short_filters(jax.random.fold_in(key_list[5], 71), 0)
    long_filter = centred(key_list[4], (LTAP, CH), LTAP ** -0.5, 0.5, ((1, 512),))
    return dict(streams=streams, cotangent=cotangent, counts=counts, short_filters=short_filters, long_filter=long_filter)


def causal_long(lead, filt, length):
    reach = filt.shape[0] - 1

    def add_tap(tap_index, total):
        piece = lax.dynamic_slice_in_dim(lead, reach - tap_index, length, 0)
        return total + filt[tap_index].astype(jnp.float32)[None, :] * piece.astype(jnp.float32)
    return lax.fori_loop(0, filt.shape[0], add_tap, jnp.zeros((length, filt.shape[1]), jnp.float32))

def anticausal_long(trail, filt, length):

    def add_tap(tap_index, total):
        piece = lax.dynamic_slice_in_dim(trail, tap_index, length, 0)
        return total + filt[tap_index].astype(jnp.float32)[None, :] * piece.astype(jnp.float32)
    return lax.fori_loop(0, filt.shape[0], add_tap, jnp.zeros((length, filt.shape[1]), jnp.float32))

def tap_products(lead, grad_rows, taps):
    reach = taps - 1
    length = grad_rows.shape[0]

    def one_tap(tap_index):
        piece = lax.dynamic_slice_in_dim(lead, reach - tap_index, length, 0)
        return lax.optimization_barrier(jnp.sum(grad_rows.astype(jnp.float32) * piece.astype(jnp.float32), axis=0))
    return lax.map(one_tap, jnp.arange(taps, dtype=jnp.int32))

def short_forward(leading, filters, length):
    taps = filters.shape[1]
    summed = jnp.zeros((filters.shape[0], length, filters.shape[2]), jnp.float32)
    for tap_index in range(taps):
        start = taps - 1 - tap_index
        summed = summed + filters[:, tap_index][:, None, :].astype(jnp.float32) * leading[:, start:start + length].astype(jnp.float32)
    return summed

def short_backward(trailing, filters, length):
    taps = filters.shape[1]
    summed = jnp.zeros((filters.shape[0], length, filters.shape[2]), jnp.float32)
    for tap_index in range(taps):
        summed = summed + filters[:, tap_index][:, None, :].astype(jnp.float32) * trailing[:, tap_index:tap_index + length].astype(jnp.float32)
    return summed

def reference(streams, cotangent, counts, short_filters, long_filter):
    reach = LTAP - 1
    short_reach = STAP - 1

    def one_window(items):
        stream, grad_out, live_count = items
        offsets = jnp.cumsum(live_count) - live_count
        slot_ids = jnp.arange(CAP, dtype=jnp.int32)
        where_to = jnp.where(slot_ids[None, :] < live_count[:, None], offsets[:, None] + slot_ids[None, :], SEQ_LEN).reshape(-1).astype(jnp.int32)
        packed = jnp.zeros((3, SEQ_LEN, CH), jnp.bfloat16).at[:, where_to].set(stream, mode='drop')
        packed_dy = jnp.zeros((SEQ_LEN, CH), jnp.bfloat16).at[where_to].set(grad_out, mode='drop')
        leading = jnp.concatenate([jnp.zeros((3, short_reach, CH), jnp.bfloat16), packed], axis=1)
        feats = short_forward(leading, short_filters, SEQ_LEN)
        query, keys, values = (feats[0], feats[1], feats[2])
        gated = (keys * values).astype(jnp.bfloat16)
        gated_lead = jnp.concatenate([jnp.zeros((reach, CH), jnp.bfloat16), gated], axis=0)
        long_out = causal_long(gated_lead, long_filter, SEQ_LEN)
        grad_query = (packed_dy * long_out).astype(jnp.bfloat16)
        grad_long = (packed_dy * query).astype(jnp.bfloat16)
        trailing = jnp.concatenate([grad_long, jnp.zeros((reach, CH), jnp.bfloat16)], axis=0)
        grad_gated = anticausal_long(trailing, long_filter, SEQ_LEN)
        grad_keys = (grad_gated * values).astype(jnp.bfloat16)
        grad_values = (grad_gated * keys).astype(jnp.bfloat16)
        grads = jnp.stack([grad_query, grad_keys, grad_values])
        grad_trail = jnp.concatenate([grads, jnp.zeros((3, short_reach, CH), jnp.bfloat16)], axis=1)
        back = short_backward(grad_trail, short_filters, SEQ_LEN).astype(jnp.bfloat16)
        long_term = tap_products(gated_lead, grad_long, LTAP)
        short_terms = []
        for tap_index in range(STAP):
            start = short_reach - tap_index
            short_terms.append(lax.optimization_barrier(jnp.sum(grads.astype(jnp.float32) * leading[:, start:start + SEQ_LEN].astype(jnp.float32), axis=1)))
        short_term = jnp.stack(short_terms, axis=1)
        back_rows = jnp.concatenate([back, jnp.zeros((3, 1, CH), jnp.bfloat16)], axis=1)
        return (back_rows[:, where_to], long_term, short_term)
    slots_out, long_terms, short_terms = lax.map(one_window, (jnp.transpose(streams, (1, 0, 2, 3)), cotangent, counts))
    stream_grads = jnp.transpose(slots_out, (1, 0, 2, 3))
    long_raw = lax.optimization_barrier(jnp.sum(long_terms, axis=0))
    short_raw = lax.optimization_barrier(jnp.sum(short_terms, axis=0))
    total = jnp.sum(long_raw * long_raw) + jnp.sum(short_raw * short_raw)
    rms = jnp.sqrt(total / float((LTAP + 3 * STAP) * CH) + 1e-06)
    return (stream_grads, long_raw / rms, short_raw / rms)
```

```python
import jax
import jax.numpy as jnp
import numpy as np
from jax import lax
from jax.experimental import pallas as pl
from jax.experimental.pallas import tpu as pltpu
from jax.sharding import PartitionSpec as P

LTAP = 128
STAP = 7
BLK = 128
FREQ = 2 * BLK
DEAD = 2.0**100
F32 = jnp.float32
BF16 = jnp.bfloat16


def split_np(matrix):
    high = matrix.astype(jnp.bfloat16)
    low = (matrix - high.astype(np.float64)).astype(jnp.bfloat16)
    return high, low


def dft_tables():
    n = np.arange(BLK)[:, None]
    k = np.arange(BLK)[None, :]
    angle = 2.0 * np.pi * ((n * k) % FREQ) / FREQ
    cosines, sines = np.cos(angle), -np.sin(angle)
    nyquist = np.where(n % 2 == 0, 1.0, -1.0)
    sines[:, :1] = nyquist
    forward = np.concatenate([cosines, sines], axis=1)
    weight = np.full((FREQ, 1), 2.0 / FREQ)
    weight[0] = weight[BLK] = 1.0 / FREQ
    backward = forward.T * weight
    return split_np(forward), split_np(backward)


def split2(x):
    high = x.astype(BF16)
    return high, (x - high.astype(F32)).astype(BF16)


def mm(a, b):
    return jnp.dot(a, b, preferred_element_type=F32)


def mm_nt(a, b):
    return lax.dot_general(a, b, (((1,), (1,)), ((), ())), preferred_element_type=F32)


def identity(size):
    rows = lax.broadcasted_iota(jnp.int32, (size, size), 0)
    cols = lax.broadcasted_iota(jnp.int32, (size, size), 1)
    return jnp.where(rows == cols, 1.0, 0.0).astype(BF16)


def turn_out_kernel(count_ref, s_ref, d_ref, o_ref):
    slots = s_ref.shape[2]
    channels = s_ref.shape[3]
    count = count_ref[0, 0]
    wide = min(256, channels)
    eye = identity(wide)
    for part in range(4):
        for at in range(0, slots, 64):
            rows = s_ref[part, 0, at : at + 64, :] if part < 3 else d_ref[0, at : at + 64, :]
            lane = lax.broadcasted_iota(jnp.int32, (wide, 64), 1) + at
            for c in range(0, channels, wide):
                turned = mm_nt(eye, rows[:, c : c + wide])
                kept = jnp.where(lane < count, turned, 0.0 if part < 3 else DEAD)
                first = part * slots + at
                o_ref[c : c + wide, first : first + 64] = kept.astype(BF16)


def turn_back_kernel(count_ref, r_ref, o_ref):
    slots = o_ref.shape[2]
    channels = o_ref.shape[3]
    count = count_ref[0, 0]
    eye = identity(64)
    for part in range(3):
        for at in range(0, slots, 64):
            first = part * slots + at
            turned = mm_nt(eye, r_ref[:, first : first + 64])
            row = lax.broadcasted_iota(jnp.int32, (64, channels), 0) + at
            o_ref[part, 0, at : at + 64, :] = jnp.where(row < count, turned, 0.0).astype(BF16)


def core_kernel(
    off_ref, r_ref, h_ref, w_ref, fh_ref, fl_ref, gh_ref, gl_ref,
    o_ref, graw_ref,
    x_ref, k_ref, v_ref, z_ref, d_ref, az_ref, ad_ref, dm_ref, out_ref,
):
    pieces, chans, _ = r_ref.shape
    slots = r_ref.shape[2] // 4
    nb = z_ref.shape[0]
    lane = lax.broadcasted_iota(jnp.int32, (chans, BLK), 1)

    x_ref[...] = jnp.zeros(x_ref.shape, F32)

    def place(offset, part):
        aligned = part * slots // BLK * BLK
        base = offset - (part * slots - aligned)
        return aligned, lax.shift_right_arithmetic(base, 7) + 1, lax.bitwise_and(base, 127)

    def pack(j, carry):
        offset = off_ref[j]
        for part in range(4):
            aligned, block, turn = place(offset, part)
            skip = part * slots - aligned
            rolled = []
            for n in range(3):
                piece = r_ref[j, :, aligned + n * BLK : aligned + (n + 1) * BLK].astype(F32)
                if part == 3:
                    piece = jnp.where(piece > 2.0**50, 0.0, piece)
                if n * BLK < skip:
                    piece = jnp.where(lane >= skip - n * BLK, piece, 0.0)
                if (n + 1) * BLK > skip + slots:
                    piece = jnp.where(lane < skip + slots - n * BLK, piece, 0.0)
                rolled.append(pltpu.roll(piece, turn, 1))
            early = lane < turn
            x_ref[part, block] += jnp.where(early, 0.0, rolled[0])
            x_ref[part, block + 1] += jnp.where(early, rolled[0], rolled[1])
            x_ref[part, block + 2] += jnp.where(early, rolled[1], rolled[2])
            x_ref[part, block + 3] += jnp.where(early, rolled[2], 0.0)
        return carry

    lax.fori_loop(0, pieces, pack, 0)

    def features(b, carry):
        feats = []
        for m in range(3):
            before, here = x_ref[m, b], x_ref[m, b + 1]
            total = w_ref[m * STAP] * here
            for i in range(1, STAP):
                moved = pltpu.roll(jnp.where(lane >= BLK - i, before, here), i, 1)
                total = total + w_ref[m * STAP + i] * moved
            feats.append(total)
        k_ref[b] = feats[1]
        v_ref[b] = feats[2]
        z_ref[b] = (feats[1] * feats[2]).astype(BF16)
        d_ref[b] = (x_ref[3, b + 1] * feats[0]).astype(BF16)
        return carry

    lax.fori_loop(0, nb, features, 0)

    step = 16
    az_ref[0] = jnp.zeros((chans, FREQ), F32)
    ad_ref[nb] = jnp.zeros((chans, FREQ), F32)

    def spectra(c, carry):
        at = c * step
        zs = z_ref[pl.ds(at, step)].reshape(step * chans, BLK)
        ds = d_ref[pl.ds(at, step)].reshape(step * chans, BLK)
        fh, fl = fh_ref[...], fl_ref[...]
        az_ref[pl.ds(at + 1, step)] = (mm(zs, fh) + mm(zs, fl)).reshape(step, chans, FREQ)
        ad_ref[pl.ds(at, step)] = (mm(ds, fh) + mm(ds, fl)).reshape(step, chans, FREQ)
        return carry

    lax.fori_loop(0, nb // step, spectra, 0)

    sign = 1.0 - 2.0 * lax.bitwise_and(
        lax.broadcasted_iota(jnp.int32, (1, 1, FREQ), 2), 1
    ).astype(F32)
    chunk = 8

    def turn(re, im):
        spectrum = jnp.concatenate([re, im], axis=2).reshape(-1, FREQ)
        high, low = split2(spectrum)
        gh, gl = gh_ref[...], gl_ref[...]
        result = mm(high, gh) + (mm(low, gh) + mm(high, gl))
        return result.reshape(-1, chans, BLK)

    def long(c, carry):
        p1, p2, p3 = carry
        at = c * chunk
        hre, him, hny = h_ref[0][None], h_ref[1][None], h_ref[2][None]
        window = az_ref[pl.ds(at + 1, chunk)] + sign * az_ref[pl.ds(at, chunk)]
        zre, zim = window[:, :, :BLK], window[:, :, BLK:]
        own = ad_ref[pl.ds(at, chunk)]
        ore, oim = own[:, :, :BLK], own[:, :, BLK:]
        both = own + sign * ad_ref[pl.ds(at + 1, chunk)]
        dre, dim = both[:, :, :BLK], both[:, :, BLK:]
        y = turn(zre * hre - zim * him, zim * hny + zre * him)
        dz = turn(dre * hre + dim * him, dim * hny - dre * him)
        dm_ref[0, pl.ds(at, chunk)] = (x_ref[3, pl.ds(at + 1, chunk)] * y).astype(BF16).astype(F32)
        dm_ref[1, pl.ds(at, chunk)] = (dz * v_ref[pl.ds(at, chunk)]).astype(BF16).astype(F32)
        dm_ref[2, pl.ds(at, chunk)] = (dz * k_ref[pl.ds(at, chunk)]).astype(BF16).astype(F32)
        p1 = p1 + jnp.sum(ore * zre, axis=0)
        p2 = p2 + jnp.sum(oim * zim, axis=0)
        p3 = p3 + jnp.sum(oim * zre - ore * zim, axis=0)
        return p1, p2, p3

    zero = jnp.zeros((chans, BLK), F32)
    p1, p2, p3 = lax.fori_loop(0, nb // chunk, long, (zero, zero, zero))
    lre = p1 + jnp.where(lane == 0, 0.0, p2)
    lim = jnp.where(lane == 0, p2, p3)
    graw_ref[0] = turn(lre[None], lim[None])[0]

    dm_ref[:, nb] = jnp.zeros((3, chans, BLK), F32)
    out_ref[:, 0] = jnp.zeros((3, chans, BLK), F32)
    for extra in range(nb + 1, out_ref.shape[1]):
        out_ref[:, extra] = jnp.zeros((3, chans, BLK), F32)
    shorts = zero
    for m in range(3):

        def back(b, sums, m=m):
            here, after, stream = dm_ref[m, b], dm_ref[m, b + 1], x_ref[m, b + 1]
            total = w_ref[m * STAP] * here
            fresh = [sums[0] + stream * here]
            for i in range(1, STAP):
                moved = pltpu.roll(jnp.where(lane < i, after, here), BLK - i, 1)
                total = total + w_ref[m * STAP + i] * moved
                fresh.append(sums[i] + stream * moved)
            out_ref[m, b + 1] = total
            return tuple(fresh)

        sums = lax.fori_loop(0, nb, back, (zero,) * STAP)
        for i in range(STAP):
            column = jnp.sum(sums[i], axis=1, keepdims=True)
            shorts = jnp.where(lane == m * STAP + i, column, shorts)
    graw_ref[1] = shorts

    def unpack(j, carry):
        offset = off_ref[j]
        kept = []
        for part in range(3):
            aligned, block, turned = place(offset, part)
            back_by = lax.bitwise_and(BLK - turned, 127)
            early = lane < turned
            for n in range(3):
                both = jnp.where(early, out_ref[part, block + n + 1], out_ref[part, block + n])
                kept.append(pltpu.roll(both, back_by, 1))
        shared = jnp.where(lane < 64, kept[2], kept[3])
        blocks = [kept[0], kept[1], shared, kept[4], kept[5], kept[6], kept[7], kept[8]]
        for n, block in enumerate(blocks):
            o_ref[j, :, n * BLK : (n + 1) * BLK] = block.astype(BF16)
        return carry

    lax.fori_loop(0, pieces, unpack, 0)


def solution(mesh):
    ctx = mesh.shape["ctx"]
    everyone = mesh.size
    (fh, fl), (gh, gl) = dft_tables()
    smem = pl.BlockSpec(memory_space=pltpu.SMEM)
    vmem = pl.BlockSpec(memory_space=pltpu.VMEM)

    def local(streams, cotangent, counts, short_filters, long_filter):
        slots, channels = streams.shape[2:]
        own = channels // ctx
        length = 8192
        nb = length // BLK
        total_params = float((LTAP + 3 * STAP) * channels * mesh.shape["dp"])

        turned = pl.pallas_call(
            turn_out_kernel,
            out_shape=jax.ShapeDtypeStruct((channels, 4 * slots), BF16),
            in_specs=[smem, vmem, vmem],
            out_specs=vmem,
            name="turn_out",
        )(counts, streams, cotangent)
        pieces = lax.all_to_all(
            turned.reshape(ctx, own, 4 * slots), "ctx", 0, 0, tiled=True
        )
        marks = pieces[:, 0, 3 * slots :].astype(F32) < 2.0**50
        live = jnp.sum(marks.astype(jnp.int32), axis=1)
        order = jnp.arange(ctx, dtype=jnp.int32)
        offsets = jnp.sum(jnp.where(order[None, :] < order[:, None], live[None, :], 0), axis=1)

        taps = long_filter.T
        spectrum = mm(taps, jnp.asarray(fh)) + mm(taps, jnp.asarray(fl))
        first = jnp.arange(BLK)[None, :] == 0
        hre, him = spectrum[:, :BLK], spectrum[:, BLK:]
        filters = jnp.stack([hre, jnp.where(first, 0.0, him), jnp.where(first, him, hre)])
        weights = jnp.broadcast_to(
            short_filters.reshape(3 * STAP, own, 1).astype(F32), (3 * STAP, own, BLK)
        )

        padded = nb + 4
        grads, raw = pl.pallas_call(
            core_kernel,
            out_shape=(
                jax.ShapeDtypeStruct((ctx, own, 8 * BLK), BF16),
                jax.ShapeDtypeStruct((2, own, BLK), F32),
            ),
            in_specs=[smem] + [vmem] * 7,
            out_specs=(vmem, vmem),
            scratch_shapes=[
                pltpu.VMEM((4, padded, own, BLK), F32),
                pltpu.VMEM((nb, own, BLK), F32),
                pltpu.VMEM((nb, own, BLK), F32),
                pltpu.VMEM((nb, own, BLK), BF16),
                pltpu.VMEM((nb, own, BLK), BF16),
                pltpu.VMEM((nb + 1, own, FREQ), F32),
                pltpu.VMEM((nb + 1, own, FREQ), F32),
                pltpu.VMEM((3, nb + 1, own, BLK), F32),
                pltpu.VMEM((3, padded, own, BLK), F32),
            ],
            compiler_params=pltpu.CompilerParams(vmem_limit_bytes=40 << 20),
            name="core",
        )(
            offsets, pieces, filters, weights,
            jnp.asarray(fh), jnp.asarray(fl), jnp.asarray(gh), jnp.asarray(gl),
        )

        squares = jnp.sum(raw * raw)
        shared = lax.all_to_all(
            jnp.broadcast_to(squares, (everyone, 1, BLK)), ("dp", "ctx"), 0, 0, tiled=True
        )
        back = lax.all_to_all(grads, "ctx", 0, 0, tiled=True)
        stream_grads = pl.pallas_call(
            turn_back_kernel,
            out_shape=jax.ShapeDtypeStruct((3, 1, slots, channels), BF16),
            in_specs=[smem, vmem],
            out_specs=vmem,
            name="turn_back",
        )(counts, back.reshape(channels, 8 * BLK))

        rms = jnp.sqrt(jnp.sum(shared[:, 0, 0]) / total_params + 1e-06)
        long_grad = (raw[0] / rms).T
        short_grad = (raw[1, :, : 3 * STAP] / rms).T.reshape(3, STAP, own)
        return stream_grads, long_grad, short_grad

    return jax.shard_map(
        local,
        mesh=mesh,
        in_specs=(
            P(None, None, "ctx", "dp"),
            P(None, "ctx", "dp"),
            P(None, "ctx"),
            P(None, None, ("dp", "ctx")),
            P(None, ("dp", "ctx")),
        ),
        out_specs=(
            P(None, None, "ctx", "dp"),
            P(None, ("dp", "ctx")),
            P(None, None, ("dp", "ctx")),
        ),
        check_vma=False,
    )
```

```python
import jax
import jax.numpy as jnp
import numpy as np
from jax import lax
from jax.experimental import pallas as pl
from jax.experimental.pallas import tpu as pltpu
from jax.sharding import Mesh
from jax.sharding import PartitionSpec as P

LTAP = 128
STAP = 7
BLK = 128
FREQ = 2 * BLK
DEAD = 2.0**100
F32 = jnp.float32
BF16 = jnp.bfloat16
DP = ("z", "core")
CTX = ("x", "y")


def split_np(matrix):
    high = matrix.astype(jnp.bfloat16)
    low = (matrix - high.astype(np.float64)).astype(jnp.bfloat16)
    return high, low


def dft_tables():
    n = np.arange(BLK)[:, None]
    k = np.arange(BLK)[None, :]
    angle = 2.0 * np.pi * ((n * k) % FREQ) / FREQ
    cosines, sines = np.cos(angle), -np.sin(angle)
    nyquist = np.where(n % 2 == 0, 1.0, -1.0)
    sines[:, :1] = nyquist
    forward = np.concatenate([cosines, sines], axis=1)
    weight = np.full((FREQ, 1), 2.0 / FREQ)
    weight[0] = weight[BLK] = 1.0 / FREQ
    backward = forward.T * weight
    return split_np(forward), split_np(backward)


def split2(x):
    high = x.astype(BF16)
    return high, (x - high.astype(F32)).astype(BF16)


def mm(a, b):
    return jnp.dot(a, b, preferred_element_type=F32)


def mm_nt(a, b):
    return lax.dot_general(a, b, (((1,), (1,)), ((), ())), preferred_element_type=F32)


def identity(size):
    rows = lax.broadcasted_iota(jnp.int32, (size, size), 0)
    cols = lax.broadcasted_iota(jnp.int32, (size, size), 1)
    return jnp.where(rows == cols, 1.0, 0.0).astype(BF16)


def turn_out_kernel(count_ref, s_ref, d_ref, o_ref):
    slots = s_ref.shape[2]
    channels = s_ref.shape[3]
    count = count_ref[0, 0]
    wide = min(256, channels)
    eye = identity(wide)
    for part in range(4):
        for at in range(0, slots, 64):
            rows = s_ref[part, 0, at : at + 64, :] if part < 3 else d_ref[0, at : at + 64, :]
            lane = lax.broadcasted_iota(jnp.int32, (wide, 64), 1) + at
            for c in range(0, channels, wide):
                turned = mm_nt(eye, rows[:, c : c + wide])
                kept = jnp.where(lane < count, turned, 0.0 if part < 3 else DEAD)
                first = part * slots + at
                o_ref[c : c + wide, first : first + 64] = kept.astype(BF16)


def turn_back_kernel(count_ref, r_ref, o_ref):
    slots = o_ref.shape[2]
    channels = o_ref.shape[3]
    count = count_ref[0, 0]
    eye = identity(64)
    for part in range(3):
        for at in range(0, slots, 64):
            first = part * slots + at
            turned = mm_nt(eye, r_ref[:, first : first + 64])
            row = lax.broadcasted_iota(jnp.int32, (64, channels), 0) + at
            o_ref[part, 0, at : at + 64, :] = jnp.where(row < count, turned, 0.0).astype(BF16)


def core_kernel(
    off_ref, r_ref, h_ref, w_ref, f_ref, g_ref,
    o_ref, graw_ref,
    x_ref, k_ref, v_ref, z_ref, d_ref, az_ref, ad_ref, dm_ref, out_ref,
):
    pieces, chans, _ = r_ref.shape
    slots = r_ref.shape[2] // 4
    nb = z_ref.shape[0]
    lane = lax.broadcasted_iota(jnp.int32, (chans, BLK), 1)

    none = jnp.zeros((chans, BLK), BF16)
    x_ref[...] = jnp.zeros(x_ref.shape, BF16)

    def place(offset, part):
        aligned = part * slots // BLK * BLK
        base = offset - (part * slots - aligned)
        return aligned, lax.shift_right_arithmetic(base, 7) + 1, lax.bitwise_and(base, 127)

    def pack(j, carry):
        offset = off_ref[j]
        for part in range(4):
            aligned, block, turn = place(offset, part)
            skip = part * slots - aligned
            rolled = []
            for n in range(3):
                piece = r_ref[j, :, aligned + n * BLK : aligned + (n + 1) * BLK]
                if part == 3:
                    piece = jnp.where(piece > 2.0**50, none, piece)
                if n * BLK < skip:
                    piece = jnp.where(lane >= skip - n * BLK, piece, none)
                if (n + 1) * BLK > skip + slots:
                    piece = jnp.where(lane < skip + slots - n * BLK, piece, none)
                rolled.append(pltpu.roll(piece, turn, 1))
            early = lane < turn
            x_ref[part, block] += jnp.where(early, none, rolled[0])
            x_ref[part, block + 1] += jnp.where(early, rolled[0], rolled[1])
            x_ref[part, block + 2] += jnp.where(early, rolled[1], rolled[2])
            x_ref[part, block + 3] += jnp.where(early, rolled[2], none)
        return carry

    lax.fori_loop(0, pieces, pack, 0, unroll=2)

    def later(before, here, i):
        return pltpu.roll(jnp.where(lane >= BLK - i, before, here), i, 1)

    def sooner(here, after, i):
        return pltpu.roll(jnp.where(lane < i, after, here), BLK - i, 1)

    def weighted(m, first, moved):
        total = w_ref[m * STAP + first] * moved[0]
        for i in range(1, min(len(moved), STAP - first)):
            total = total + w_ref[m * STAP + first + i] * moved[i]
        return total

    zero = jnp.zeros((chans, BLK), F32)

    def features(b, carried):
        feats, kept = [], []
        for m in range(3):
            before, here = x_ref[m, b], x_ref[m, b + 1]
            moved = [here.astype(F32)] + [later(before, here, i).astype(F32) for i in (1, 2, 3)]
            far = weighted(m, 4, moved)
            feats.append(weighted(m, 0, moved) + later(carried[m], far, 4))
            kept.append(far)
        k_ref[b] = feats[1]
        v_ref[b] = feats[2]
        z_ref[b] = (feats[1] * feats[2]).astype(BF16)
        d_ref[b] = (x_ref[3, b + 1].astype(F32) * feats[0]).astype(BF16)
        return tuple(kept)

    lax.fori_loop(0, nb, features, (zero,) * 3, unroll=4)

    step = 16
    az_ref[0] = jnp.zeros((chans, FREQ), F32)
    ad_ref[nb] = jnp.zeros((chans, FREQ), F32)

    def spectra(c, carry):
        at = c * step
        zs = z_ref[pl.ds(at, step)].reshape(step * chans, BLK)
        ds = d_ref[pl.ds(at, step)].reshape(step * chans, BLK)
        table = f_ref[...]
        for source, to, first in ((zs, az_ref, at + 1), (ds, ad_ref, at)):
            result = mm(jnp.concatenate([source, source], axis=1), table)
            to[pl.ds(first, step)] = result.reshape(step, chans, FREQ)
        return carry

    lax.fori_loop(0, nb // step, spectra, 0)

    sign = 1.0 - 2.0 * lax.bitwise_and(
        lax.broadcasted_iota(jnp.int32, (1, 1, FREQ), 2), 1
    ).astype(F32)
    chunk = 8

    def turn(re, im):
        rehi, relo = split2(re.reshape(-1, BLK))
        imhi, imlo = split2(im.reshape(-1, BLK))
        wide = jnp.concatenate([rehi, imhi, relo, imlo, rehi, imhi], axis=1)
        return mm(wide, g_ref[...]).reshape(-1, chans, BLK)

    def long(c, carry):
        p1, p2, p3 = carry
        at = c * chunk
        hre, him, hny = h_ref[0][None], h_ref[1][None], h_ref[2][None]
        window = az_ref[pl.ds(at + 1, chunk)] + sign * az_ref[pl.ds(at, chunk)]
        zre, zim = window[:, :, :BLK], window[:, :, BLK:]
        own = ad_ref[pl.ds(at, chunk)]
        ore, oim = own[:, :, :BLK], own[:, :, BLK:]
        p1 = p1 + jnp.sum(ore * zre, axis=0)
        p2 = p2 + jnp.sum(oim * zim, axis=0)
        p3 = p3 + jnp.sum(oim * zre - ore * zim, axis=0)
        y = turn(zre * hre - zim * him, zim * hny + zre * him)
        dm_ref[0, pl.ds(at, chunk)] = (x_ref[3, pl.ds(at + 1, chunk)].astype(F32) * y).astype(BF16)
        both = own + sign * ad_ref[pl.ds(at + 1, chunk)]
        dre, dim = both[:, :, :BLK], both[:, :, BLK:]
        dz = turn(dre * hre + dim * him, dim * hny - dre * him)
        dm_ref[1, pl.ds(at, chunk)] = (dz * v_ref[pl.ds(at, chunk)]).astype(BF16)
        dm_ref[2, pl.ds(at, chunk)] = (dz * k_ref[pl.ds(at, chunk)]).astype(BF16)
        return p1, p2, p3

    p1, p2, p3 = lax.fori_loop(0, nb // chunk, long, (zero, zero, zero))
    lre = p1 + jnp.where(lane == 0, 0.0, p2)
    lim = jnp.where(lane == 0, p2, p3)
    graw_ref[0] = turn(lre[None], lim[None])[0]

    dm_ref[:, nb] = jnp.zeros((3, chans, BLK), BF16)
    out_ref[:, 0] = jnp.zeros((3, chans, BLK), BF16)
    for extra in range(nb + 1, out_ref.shape[1]):
        out_ref[:, extra] = jnp.zeros((3, chans, BLK), BF16)
    shorts = zero
    for m in range(3):

        def back(n, carried, m=m):
            sums, far_after = carried
            b = nb - 1 - n
            here, after, stream = dm_ref[m, b], dm_ref[m, b + 1], x_ref[m, b + 1]
            old = later(x_ref[m, b], stream, 4).astype(F32)
            stream = stream.astype(F32)
            moved = [here.astype(F32)] + [sooner(here, after, i).astype(F32) for i in (1, 2, 3)]
            far = weighted(m, 4, moved)
            out_ref[m, b + 1] = (weighted(m, 0, moved) + sooner(far, far_after, 4)).astype(BF16)
            fresh = [sums[i] + stream * moved[i] for i in range(4)]
            fresh += [sums[4 + i] + old * moved[i] for i in range(3)]
            return tuple(fresh), far

        sums, _ = lax.fori_loop(0, nb, back, ((zero,) * STAP, zero), unroll=4)
        for i in range(STAP):
            column = jnp.sum(sums[i], axis=1, keepdims=True)
            shorts = jnp.where(lane == m * STAP + i, column, shorts)
    graw_ref[1] = shorts

    def unpack(j, carry):
        offset = off_ref[j]
        kept = []
        for part in range(3):
            aligned, block, turned = place(offset, part)
            back_by = lax.bitwise_and(BLK - turned, 127)
            early = lane < turned
            for n in range(3):
                both = jnp.where(early, out_ref[part, block + n + 1], out_ref[part, block + n])
                kept.append(pltpu.roll(both, back_by, 1))
        shared = jnp.where(lane < 64, kept[2], kept[3])
        blocks = [kept[0], kept[1], shared, kept[4], kept[5], kept[6], kept[7], kept[8]]
        for n, block in enumerate(blocks):
            o_ref[j, :, n * BLK : (n + 1) * BLK] = block
        return carry

    lax.fori_loop(0, pieces, unpack, 0, unroll=2)


def solution(mesh):
    ctx = mesh.shape["ctx"]
    cores = min(2, mesh.shape["dp"])
    finer = Mesh(mesh.devices.reshape(-1, cores, 4, ctx // 4), ("z", "core", "x", "y"))
    (fh, fl), (gh, gl) = dft_tables()
    forward = np.concatenate([fh, fl])
    backward = np.concatenate([gh, gh, gl])
    smem = pl.BlockSpec(memory_space=pltpu.SMEM)
    vmem = pl.BlockSpec(memory_space=pltpu.VMEM)

    def local(streams, cotangent, counts, short_filters, long_filter):
        slots, channels = streams.shape[2:]
        own = channels // ctx
        length = 8192
        nb = length // BLK
        total_params = float((LTAP + 3 * STAP) * channels * mesh.shape["dp"])

        turned = pl.pallas_call(
            turn_out_kernel,
            out_shape=jax.ShapeDtypeStruct((channels, 4 * slots), BF16),
            in_specs=[smem, vmem, vmem],
            out_specs=vmem,
            name="turn_out",
        )(counts, streams, cotangent)
        pieces = lax.all_to_all(
            turned.reshape(ctx, own, 4 * slots), CTX, 0, 0, tiled=True
        )
        marks = pieces[:, 0, 3 * slots :].astype(F32) < 2.0**50
        live = jnp.sum(marks.astype(jnp.int32), axis=1)
        order = jnp.arange(ctx, dtype=jnp.int32)
        offsets = jnp.sum(jnp.where(order[None, :] < order[:, None], live[None, :], 0), axis=1)

        taps = long_filter.T
        spectrum = mm(jnp.concatenate([taps, taps], axis=1), jnp.asarray(forward))
        first = jnp.arange(BLK)[None, :] == 0
        hre, him = spectrum[:, :BLK], spectrum[:, BLK:]
        filters = jnp.stack([hre, jnp.where(first, 0.0, him), jnp.where(first, him, hre)])
        weights = jnp.broadcast_to(
            short_filters.reshape(3 * STAP, own, 1).astype(F32), (3 * STAP, own, BLK)
        )

        padded = nb + 4
        grads, raw = pl.pallas_call(
            core_kernel,
            out_shape=(
                jax.ShapeDtypeStruct((ctx, own, 8 * BLK), BF16),
                jax.ShapeDtypeStruct((2, own, BLK), F32),
            ),
            in_specs=[smem] + [vmem] * 5,
            out_specs=(vmem, vmem),
            scratch_shapes=[
                pltpu.VMEM((4, padded, own, BLK), BF16),
                pltpu.VMEM((nb, own, BLK), F32),
                pltpu.VMEM((nb, own, BLK), F32),
                pltpu.VMEM((nb, own, BLK), BF16),
                pltpu.VMEM((nb, own, BLK), BF16),
                pltpu.VMEM((nb + 1, own, FREQ), F32),
                pltpu.VMEM((nb + 1, own, FREQ), F32),
                pltpu.VMEM((3, nb + 1, own, BLK), BF16),
                pltpu.VMEM((3, padded, own, BLK), BF16),
            ],
            compiler_params=pltpu.CompilerParams(vmem_limit_bytes=40 << 20),
            name="core",
        )(
            offsets, pieces, filters, weights, jnp.asarray(forward), jnp.asarray(backward),
        )

        squares = jnp.sum(raw * raw)
        back = lax.all_to_all(grads, CTX, 0, 0, tiled=True)
        shared = jnp.broadcast_to(squares, (1, BLK))
        for axis in ("core", "z", "x"):
            shared = jnp.sum(lax.all_gather(shared, axis, axis=0, tiled=True), axis=0, keepdims=True)
        shared, back = lax.optimization_barrier((shared, back))
        rows = lax.axis_size("y")
        shared = lax.all_to_all(jnp.broadcast_to(shared, (rows, BLK)), "y", 0, 0, tiled=True)
        stream_grads = pl.pallas_call(
            turn_back_kernel,
            out_shape=jax.ShapeDtypeStruct((3, 1, slots, channels), BF16),
            in_specs=[smem, vmem],
            out_specs=vmem,
            name="turn_back",
        )(counts, back.reshape(channels, 8 * BLK))

        rms = jnp.sqrt(jnp.sum(shared[:, 0]) / total_params + 1e-06)
        long_grad = (raw[0] / rms).T
        short_grad = (raw[1, :, : 3 * STAP] / rms).T.reshape(3, STAP, own)
        return stream_grads, long_grad, short_grad

    return jax.shard_map(
        local,
        mesh=finer,
        in_specs=(
            P(None, None, CTX, DP),
            P(None, CTX, DP),
            P(None, CTX),
            P(None, None, DP + CTX),
            P(None, DP + CTX),
        ),
        out_specs=(
            P(None, None, CTX, DP),
            P(None, DP + CTX),
            P(None, None, DP + CTX),
        ),
        check_vma=False,
    )
```

```python
import jax
import jax.numpy as jnp
import numpy as np
from jax import lax
from jax.experimental import pallas as pl
from jax.experimental.pallas import tpu as pltpu
from jax.sharding import Mesh
from jax.sharding import PartitionSpec as P

LTAP = 128
STAP = 7
BLK = 128
FREQ = 2 * BLK
DEAD = 2.0**100
F32 = jnp.float32
BF16 = jnp.bfloat16
DP = ("z", "core")
CTX = ("x", "y")


def split_np(matrix):
    high = matrix.astype(jnp.bfloat16)
    low = (matrix - high.astype(np.float64)).astype(jnp.bfloat16)
    return high, low


def dft_tables():
    n = np.arange(BLK)[:, None]
    k = np.arange(BLK)[None, :]
    angle = 2.0 * np.pi * ((n * k) % FREQ) / FREQ
    cosines, sines = np.cos(angle), -np.sin(angle)
    nyquist = np.where(n % 2 == 0, 1.0, -1.0)
    sines[:, :1] = nyquist
    forward = np.concatenate([cosines, sines], axis=1)
    weight = np.full((FREQ, 1), 2.0 / FREQ)
    weight[0] = weight[BLK] = 1.0 / FREQ
    backward = forward.T * weight
    return split_np(forward), split_np(backward)


def split2(x):
    high = x.astype(BF16)
    return high, (x - high.astype(F32)).astype(BF16)


def mm(a, b):
    return jnp.dot(a, b, preferred_element_type=F32)


def mm_nt(a, b):
    return lax.dot_general(a, b, (((1,), (1,)), ((), ())), preferred_element_type=F32)


def identity(size):
    rows = lax.broadcasted_iota(jnp.int32, (size, size), 0)
    cols = lax.broadcasted_iota(jnp.int32, (size, size), 1)
    return jnp.where(rows == cols, 1.0, 0.0).astype(BF16)


def turn_out_kernel(count_ref, s_ref, d_ref, o_ref):
    slots = s_ref.shape[2]
    channels = s_ref.shape[3]
    count = count_ref[0, 0]
    wide = min(256, channels)
    eye = identity(wide)
    lane = lax.broadcasted_iota(jnp.int32, (wide, BLK), 1)
    for first in range(0, 4 * slots, BLK):
        pieces, token, fill = [], lane, 0.0
        part, at = divmod(first, slots)
        fill = DEAD if part == 3 else 0.0
        rest = min(BLK, slots - at)
        token = lane + at
        for p, low, size in ((part, at, rest), (part + 1, 0, BLK - rest)):
            if size:
                pieces.append(s_ref[p, 0, low : low + size] if p < 3 else d_ref[0, low : low + size])
        if rest < BLK:
            token = jnp.where(lane < rest, token, lane - rest)
            fill = jnp.where(lane < rest, fill, DEAD if part == 2 else 0.0)
        rows = pieces[0] if len(pieces) == 1 else jnp.concatenate(pieces, axis=0)
        for c in range(0, channels, wide):
            kept = jnp.where(token < count, mm_nt(eye, rows[:, c : c + wide]), fill)
            o_ref[c : c + wide, first : first + BLK] = kept.astype(BF16)


def turn_back_kernel(count_ref, r_ref, o_ref):
    slots = o_ref.shape[2]
    channels = o_ref.shape[3]
    count = count_ref[0, 0]
    eye = identity(BLK)
    row = lax.broadcasted_iota(jnp.int32, (BLK, channels), 0)
    for first in range(0, 3 * slots, BLK):
        turned = mm_nt(eye, r_ref[:, first : first + BLK])
        part, at = divmod(first, slots)
        rest = min(BLK, slots - at)
        kept = jnp.where(row[:rest] + at < count, turned[:rest], 0.0).astype(BF16)
        o_ref[part, 0, at : at + rest] = kept
        if rest < BLK and part < 2:
            kept = jnp.where(row[: BLK - rest] < count, turned[rest:], 0.0).astype(BF16)
            o_ref[part + 1, 0, : BLK - rest] = kept


def core_kernel(
    off_ref, r_ref, h_ref, w_ref, f_ref, g_ref,
    o_ref, graw_ref, sq_ref,
    x_ref, k_ref, v_ref, z_ref, d_ref, az_ref, ad_ref, dm_ref, out_ref,
):
    pieces, chans, _ = r_ref.shape
    slots = r_ref.shape[2] // 4
    nb = z_ref.shape[0]
    lane = lax.broadcasted_iota(jnp.int32, (chans, BLK), 1)

    none = jnp.zeros((chans, BLK), BF16)
    x_ref[...] = jnp.zeros(x_ref.shape, BF16)

    def place(offset, part):
        aligned = part * slots // BLK * BLK
        base = offset - (part * slots - aligned)
        return aligned, lax.shift_right_arithmetic(base, 7) + 1, lax.bitwise_and(base, 127)

    def pack(j, carry):
        offset = off_ref[j]
        for part in range(4):
            aligned, block, turn = place(offset, part)
            skip = part * slots - aligned
            rolled = []
            for n in range(3):
                piece = r_ref[j, :, aligned + n * BLK : aligned + (n + 1) * BLK]
                if part == 3:
                    piece = jnp.where(piece > 2.0**50, none, piece)
                if n * BLK < skip:
                    piece = jnp.where(lane >= skip - n * BLK, piece, none)
                if (n + 1) * BLK > skip + slots:
                    piece = jnp.where(lane < skip + slots - n * BLK, piece, none)
                rolled.append(pltpu.roll(piece, turn, 1))
            early = lane < turn
            fresh = jnp.where(early, rolled[0], rolled[1])
            x_ref[part, block] += jnp.where(early, none, rolled[0])
            x_ref[part, block + 1] = x_ref[part, block + 1] + fresh if skip else fresh
            x_ref[part, block + 2] = jnp.where(early, rolled[1], rolled[2])
            x_ref[part, block + 3] = jnp.where(early, rolled[2], none)
        return carry

    lax.fori_loop(0, pieces, pack, 0, unroll=2)

    def later(before, here, i):
        return pltpu.roll(jnp.where(lane >= BLK - i, before, here), i, 1)

    def sooner(here, after, i):
        return pltpu.roll(jnp.where(lane < i, after, here), BLK - i, 1)

    def weighted(m, first, moved):
        total = w_ref[m * STAP + first] * moved[0]
        for i in range(1, min(len(moved), STAP - first)):
            total = total + w_ref[m * STAP + first + i] * moved[i]
        return total

    zero = jnp.zeros((chans, BLK), F32)

    for m in range(3):

        def features(b, carried, m=m):
            before, here = x_ref[m, b], x_ref[m, b + 1]
            moved = [here.astype(F32)] + [later(before, here, i).astype(F32) for i in (1, 2, 3)]
            far = weighted(m, 4, moved)
            feature = weighted(m, 0, moved) + later(carried, far, 4)
            if m == 0:
                d_ref[b] = (x_ref[3, b + 1].astype(F32) * feature).astype(BF16)
            elif m == 1:
                k_ref[b] = feature
            else:
                v_ref[b] = feature
                z_ref[b] = (k_ref[b] * feature).astype(BF16)
            return far

        lax.fori_loop(0, nb, features, zero, unroll=8)

    step = 32
    az_ref[0] = jnp.zeros((chans, FREQ), F32)
    ad_ref[nb] = jnp.zeros((chans, FREQ), F32)

    def spectra(c, carry):
        at = c * step
        zs = z_ref[pl.ds(at, step)].reshape(step * chans, BLK)
        ds = d_ref[pl.ds(at, step)].reshape(step * chans, BLK)
        table = f_ref[...]
        for source, to, first in ((zs, az_ref, at + 1), (ds, ad_ref, at)):
            result = mm(jnp.concatenate([source, source], axis=1), table)
            to[pl.ds(first, step)] = result.reshape(step, chans, FREQ)
        return carry

    lax.fori_loop(0, nb // step, spectra, 0)

    sign = 1.0 - 2.0 * lax.bitwise_and(
        lax.broadcasted_iota(jnp.int32, (1, 1, FREQ), 2), 1
    ).astype(F32)
    chunk = 16

    def turn(re, im):
        rehi, relo = split2(re.reshape(-1, BLK))
        imhi, imlo = split2(im.reshape(-1, BLK))
        wide = jnp.concatenate([rehi, imhi, relo, imlo, rehi, imhi], axis=1)
        return mm(wide, g_ref[...]).reshape(-1, chans, BLK)

    def long(c, carry):
        p1, p2, p3 = carry
        at = c * chunk
        hre, him, hny = h_ref[0][None], h_ref[1][None], h_ref[2][None]
        window = az_ref[pl.ds(at + 1, chunk)] + sign * az_ref[pl.ds(at, chunk)]
        zre, zim = window[:, :, :BLK], window[:, :, BLK:]
        own = ad_ref[pl.ds(at, chunk)]
        ore, oim = own[:, :, :BLK], own[:, :, BLK:]
        p1 = p1 + jnp.sum(ore * zre, axis=0)
        p2 = p2 + jnp.sum(oim * zim, axis=0)
        p3 = p3 + jnp.sum(oim * zre - ore * zim, axis=0)
        y = turn(zre * hre - zim * him, zim * hny + zre * him)
        dm_ref[0, pl.ds(at, chunk)] = (x_ref[3, pl.ds(at + 1, chunk)].astype(F32) * y).astype(BF16)
        both = own + sign * ad_ref[pl.ds(at + 1, chunk)]
        dre, dim = both[:, :, :BLK], both[:, :, BLK:]
        dz = turn(dre * hre + dim * him, dim * hny - dre * him)
        dm_ref[1, pl.ds(at, chunk)] = (dz * v_ref[pl.ds(at, chunk)]).astype(BF16)
        dm_ref[2, pl.ds(at, chunk)] = (dz * k_ref[pl.ds(at, chunk)]).astype(BF16)
        return p1, p2, p3

    p1, p2, p3 = lax.fori_loop(0, nb // chunk, long, (zero, zero, zero))
    lre = p1 + jnp.where(lane == 0, 0.0, p2)
    lim = jnp.where(lane == 0, p2, p3)
    longs = turn(lre[None], lim[None])[0]
    graw_ref[0] = longs

    dm_ref[:, nb] = jnp.zeros((3, chans, BLK), BF16)
    out_ref[:, 0] = jnp.zeros((3, chans, BLK), BF16)
    for extra in range(nb + 1, out_ref.shape[1]):
        out_ref[:, extra] = jnp.zeros((3, chans, BLK), BF16)
    shorts = zero
    for m in range(3):

        def back(n, carried, m=m):
            sums, far_after = carried
            b = nb - 1 - n
            here, after, stream = dm_ref[m, b], dm_ref[m, b + 1], x_ref[m, b + 1]
            old = later(x_ref[m, b], stream, 4).astype(F32)
            stream = stream.astype(F32)
            moved = [here.astype(F32)] + [sooner(here, after, i).astype(F32) for i in (1, 2, 3)]
            far = weighted(m, 4, moved)
            out_ref[m, b + 1] = (weighted(m, 0, moved) + sooner(far, far_after, 4)).astype(BF16)
            fresh = [sums[i] + stream * moved[i] for i in range(4)]
            fresh += [sums[4 + i] + old * moved[i] for i in range(3)]
            return tuple(fresh), far

        sums, _ = lax.fori_loop(0, nb, back, ((zero,) * STAP, zero), unroll=8)
        for i in range(STAP):
            column = jnp.sum(sums[i], axis=1, keepdims=True)
            shorts = jnp.where(lane == m * STAP + i, column, shorts)
    graw_ref[1] = shorts
    squares = jnp.sum(longs * longs + shorts * shorts, axis=0, keepdims=True)
    sq_ref[...] = jnp.broadcast_to(jnp.sum(squares, axis=1, keepdims=True), (1, BLK))

    def unpack(j, carry):
        offset = off_ref[j]
        kept = []
        for part in range(3):
            aligned, block, turned = place(offset, part)
            back_by = lax.bitwise_and(BLK - turned, 127)
            early = lane < turned
            for n in range(3):
                both = jnp.where(early, out_ref[part, block + n + 1], out_ref[part, block + n])
                kept.append(pltpu.roll(both, back_by, 1))
        shared = jnp.where(lane < 64, kept[2], kept[3])
        blocks = [kept[0], kept[1], shared, kept[4], kept[5], kept[6], kept[7], kept[8]]
        for n, block in enumerate(blocks):
            o_ref[j, :, n * BLK : (n + 1) * BLK] = block
        return carry

    lax.fori_loop(0, pieces, unpack, 0, unroll=2)


def solution(mesh):
    ctx = mesh.shape["ctx"]
    cores = min(2, mesh.shape["dp"])
    finer = Mesh(mesh.devices.reshape(-1, cores, 4, ctx // 4), ("z", "core", "x", "y"))
    (fh, fl), (gh, gl) = dft_tables()
    forward = np.concatenate([fh, fl])
    backward = np.concatenate([gh, gh, gl])
    smem = pl.BlockSpec(memory_space=pltpu.SMEM)
    vmem = pl.BlockSpec(memory_space=pltpu.VMEM)

    def local(streams, cotangent, counts, short_filters, long_filter):
        slots, channels = streams.shape[2:]
        own = channels // ctx
        length = 8192
        nb = length // BLK
        total_params = float((LTAP + 3 * STAP) * channels * mesh.shape["dp"])

        turned = pl.pallas_call(
            turn_out_kernel,
            out_shape=jax.ShapeDtypeStruct((channels, 4 * slots), BF16),
            in_specs=[smem, vmem, vmem],
            out_specs=vmem,
            name="turn_out",
        )(counts, streams, cotangent)
        pieces = lax.all_to_all(
            turned.reshape(ctx, own, 4 * slots), CTX, 0, 0, tiled=True
        )
        marks = pieces[:, 0, 3 * slots :].astype(F32) < 2.0**50
        live = jnp.sum(marks.astype(jnp.int32), axis=1)
        order = jnp.arange(ctx, dtype=jnp.int32)
        offsets = jnp.sum(jnp.where(order[None, :] < order[:, None], live[None, :], 0), axis=1)

        taps = long_filter.T
        spectrum = mm(jnp.concatenate([taps, taps], axis=1), jnp.asarray(forward))
        first = jnp.arange(BLK)[None, :] == 0
        hre, him = spectrum[:, :BLK], spectrum[:, BLK:]
        filters = jnp.stack([hre, jnp.where(first, 0.0, him), jnp.where(first, him, hre)])
        weights = jnp.broadcast_to(
            short_filters.reshape(3 * STAP, own, 1).astype(F32), (3 * STAP, own, BLK)
        )

        padded = nb + 4
        grads, raw, shared = pl.pallas_call(
            core_kernel,
            out_shape=(
                jax.ShapeDtypeStruct((ctx, own, 8 * BLK), BF16),
                jax.ShapeDtypeStruct((2, own, BLK), F32),
                jax.ShapeDtypeStruct((1, BLK), F32),
            ),
            in_specs=[smem] + [vmem] * 5,
            out_specs=(vmem, vmem, vmem),
            scratch_shapes=[
                pltpu.VMEM((4, padded, own, BLK), BF16),
                pltpu.VMEM((nb, own, BLK), F32),
                pltpu.VMEM((nb, own, BLK), F32),
                pltpu.VMEM((nb, own, BLK), BF16),
                pltpu.VMEM((nb, own, BLK), BF16),
                pltpu.VMEM((nb + 1, own, FREQ), F32),
                pltpu.VMEM((nb + 1, own, FREQ), F32),
                pltpu.VMEM((3, nb + 1, own, BLK), BF16),
                pltpu.VMEM((3, padded, own, BLK), BF16),
            ],
            compiler_params=pltpu.CompilerParams(vmem_limit_bytes=40 << 20),
            name="core",
        )(
            offsets, pieces, filters, weights, jnp.asarray(forward), jnp.asarray(backward),
        )

        back = lax.all_to_all(grads, CTX, 0, 0, tiled=True)
        for axis in (DP, "x"):
            shared = jnp.sum(lax.all_gather(shared, axis, axis=0, tiled=True), axis=0, keepdims=True)
        shared, back = lax.optimization_barrier((shared, back))
        rows = lax.axis_size("y")
        shared = lax.all_to_all(jnp.broadcast_to(shared, (rows, BLK)), "y", 0, 0, tiled=True)
        stream_grads = pl.pallas_call(
            turn_back_kernel,
            out_shape=jax.ShapeDtypeStruct((3, 1, slots, channels), BF16),
            in_specs=[smem, vmem],
            out_specs=vmem,
            name="turn_back",
        )(counts, back.reshape(channels, 8 * BLK))

        rms = jnp.sqrt(jnp.sum(shared[:, 0]) / total_params + 1e-06)
        long_grad = (raw[0] / rms).T
        short_grad = (raw[1, :, : 3 * STAP] / rms).T.reshape(3, STAP, own)
        return stream_grads, long_grad, short_grad

    return jax.shard_map(
        local,
        mesh=finer,
        in_specs=(
            P(None, None, CTX, DP),
            P(None, CTX, DP),
            P(None, CTX),
            P(None, None, DP + CTX),
            P(None, DP + CTX),
        ),
        out_specs=(
            P(None, None, CTX, DP),
            P(None, DP + CTX),
            P(None, None, DP + CTX),
        ),
        check_vma=False,
    )
```

```python
import jax
import jax.numpy as jnp
import numpy as np
from jax import lax
from jax.experimental import pallas as pl
from jax.experimental.pallas import tpu as pltpu
from jax.sharding import Mesh
from jax.sharding import PartitionSpec as P

LTAP = 128
STAP = 7
BLK = 128
FREQ = 2 * BLK
DEAD = 2.0**100
F32 = jnp.float32
BF16 = jnp.bfloat16
DP = ("z", "core")
CTX = ("x", "y")


def split_np(matrix):
    high = matrix.astype(jnp.bfloat16)
    low = (matrix - high.astype(np.float64)).astype(jnp.bfloat16)
    return high, low


def dft_tables():
    n = np.arange(BLK)[:, None]
    k = np.arange(BLK)[None, :]
    angle = 2.0 * np.pi * ((n * k) % FREQ) / FREQ
    cosines, sines = np.cos(angle), -np.sin(angle)
    nyquist = np.where(n % 2 == 0, 1.0, -1.0)
    sines[:, :1] = nyquist
    forward = np.concatenate([cosines, sines], axis=1)
    weight = np.full((FREQ, 1), 2.0 / FREQ)
    weight[0] = weight[BLK] = 1.0 / FREQ
    backward = forward.T * weight
    return split_np(forward), split_np(backward)


def shift_tables():
    row = np.arange(FREQ)[:, None]
    col = np.arange(BLK)[None, :]
    past = [row == BLK + col - i for i in range(1, STAP)]
    future = [row == col + i for i in range(1, STAP)]
    return tuple(np.concatenate(t, axis=1).astype(jnp.bfloat16) for t in (past, future))


def split2(x):
    high = x.astype(BF16)
    return high, (x - high.astype(F32)).astype(BF16)


def mm(a, b):
    return jnp.dot(a, b, preferred_element_type=F32)


def mm_nt(a, b):
    return lax.dot_general(a, b, (((1,), (1,)), ((), ())), preferred_element_type=F32)


def identity(size):
    rows = lax.broadcasted_iota(jnp.int32, (size, size), 0)
    cols = lax.broadcasted_iota(jnp.int32, (size, size), 1)
    return jnp.where(rows == cols, 1.0, 0.0).astype(BF16)


def turn_out_kernel(count_ref, s_ref, d_ref, o_ref):
    slots = s_ref.shape[2]
    channels = s_ref.shape[3]
    count = count_ref[0, 0]
    wide = min(256, channels)
    eye = identity(wide)
    lane = lax.broadcasted_iota(jnp.int32, (wide, BLK), 1)
    for first in range(0, 4 * slots, BLK):
        pieces, token, fill = [], lane, 0.0
        part, at = divmod(first, slots)
        fill = DEAD if part == 3 else 0.0
        rest = min(BLK, slots - at)
        token = lane + at
        for p, low, size in ((part, at, rest), (part + 1, 0, BLK - rest)):
            if size:
                pieces.append(s_ref[p, 0, low : low + size] if p < 3 else d_ref[0, low : low + size])
        if rest < BLK:
            token = jnp.where(lane < rest, token, lane - rest)
            fill = jnp.where(lane < rest, fill, DEAD if part == 2 else 0.0)
        rows = pieces[0] if len(pieces) == 1 else jnp.concatenate(pieces, axis=0)
        for c in range(0, channels, wide):
            kept = jnp.where(token < count, mm_nt(eye, rows[:, c : c + wide]), fill)
            o_ref[c : c + wide, first : first + BLK] = kept.astype(BF16)


def turn_back_kernel(count_ref, r_ref, o_ref):
    slots = o_ref.shape[2]
    channels = o_ref.shape[3]
    count = count_ref[0, 0]
    eye = identity(BLK)
    row = lax.broadcasted_iota(jnp.int32, (BLK, channels), 0)
    for first in range(0, 3 * slots, BLK):
        turned = mm_nt(eye, r_ref[:, first : first + BLK])
        part, at = divmod(first, slots)
        rest = min(BLK, slots - at)
        kept = jnp.where(row[:rest] + at < count, turned[:rest], 0.0).astype(BF16)
        o_ref[part, 0, at : at + rest] = kept
        if rest < BLK and part < 2:
            kept = jnp.where(row[: BLK - rest] < count, turned[rest:], 0.0).astype(BF16)
            o_ref[part + 1, 0, : BLK - rest] = kept


def core_kernel(
    off_ref, r_ref, h_ref, w_ref, f_ref, g_ref, fs_ref, bs_ref,
    o_ref, graw_ref, sq_ref,
    xq_ref, xk_ref, xv_ref, xd_ref, k_ref, v_ref, z_ref, d_ref, az_ref, ad_ref, dm_ref, out_ref, sum_ref,
):
    pieces, chans, _ = r_ref.shape
    slots = r_ref.shape[2] // 4
    nb = z_ref.shape[0]
    lane = lax.broadcasted_iota(jnp.int32, (chans, BLK), 1)

    none = jnp.zeros((chans, BLK), BF16)
    x_refs = (xq_ref, xk_ref, xv_ref, xd_ref)
    for ref in x_refs:
        ref[...] = jnp.zeros(ref.shape, BF16)

    def place(offset, part):
        aligned = part * slots // BLK * BLK
        base = offset - (part * slots - aligned)
        return aligned, lax.shift_right_arithmetic(base, 7) + 1, lax.bitwise_and(base, 127)

    def pack(j, carry):
        offset = off_ref[j]
        for part in range(4):
            aligned, block, turn = place(offset, part)
            skip = part * slots - aligned
            rolled = []
            for n in range(3):
                piece = r_ref[j, :, aligned + n * BLK : aligned + (n + 1) * BLK]
                if part == 3:
                    piece = jnp.where(piece > 2.0**50, none, piece)
                if n * BLK < skip:
                    piece = jnp.where(lane >= skip - n * BLK, piece, none)
                if (n + 1) * BLK > skip + slots:
                    piece = jnp.where(lane < skip + slots - n * BLK, piece, none)
                rolled.append(pltpu.roll(piece, turn, 1))
            early = lane < turn
            fresh = jnp.where(early, rolled[0], rolled[1])
            x_ref = x_refs[part]
            x_ref[block] += jnp.where(early, none, rolled[0])
            x_ref[block + 1] = x_ref[block + 1] + fresh if skip else fresh
            x_ref[block + 2] = jnp.where(early, rolled[1], rolled[2])
            x_ref[block + 3] = jnp.where(early, rolled[2], none)
        return carry

    lax.fori_loop(0, pieces, pack, 0, unroll=2)

    zero = jnp.zeros((chans, BLK), F32)
    group = 32

    def moved_blocks(first, second, table_ref):
        pairs = jnp.concatenate([first.reshape(-1, BLK), second.reshape(-1, BLK)], axis=1)
        for at in range(0, (STAP - 1) * BLK, FREQ):
            both = mm(pairs, table_ref[:, at : at + FREQ])
            yield both[:, :BLK].reshape(-1, chans, BLK)
            yield both[:, BLK:].reshape(-1, chans, BLK)

    def features(c, carry):
        at = c * group
        before = jnp.concatenate([x_refs[m][pl.ds(at, group)] for m in range(3)])
        here = jnp.concatenate([x_refs[m][pl.ds(at + 1, group)] for m in range(3)])
        feats = [
            w_ref[m * STAP][None] * here[m * group : (m + 1) * group].astype(F32) for m in range(3)
        ]
        for i, moved in enumerate(moved_blocks(before, here, fs_ref), 1):
            for m in range(3):
                feats[m] += w_ref[m * STAP + i][None] * moved[m * group : (m + 1) * group]
        k_ref[pl.ds(at, group)] = feats[1]
        v_ref[pl.ds(at, group)] = feats[2]
        z_ref[pl.ds(at, group)] = (feats[1] * feats[2]).astype(BF16)
        d_ref[pl.ds(at, group)] = (xd_ref[pl.ds(at + 1, group)].astype(F32) * feats[0]).astype(BF16)
        return carry

    lax.fori_loop(0, nb // group, features, 0)

    step = 32
    az_ref[0] = jnp.zeros((chans, FREQ), F32)
    ad_ref[nb] = jnp.zeros((chans, FREQ), F32)

    def spectra(c, carry):
        at = c * step
        zs = z_ref[pl.ds(at, step)].reshape(step * chans, BLK)
        ds = d_ref[pl.ds(at, step)].reshape(step * chans, BLK)
        table = f_ref[...]
        for source, to, first in ((zs, az_ref, at + 1), (ds, ad_ref, at)):
            result = mm(jnp.concatenate([source, source], axis=1), table)
            to[pl.ds(first, step)] = result.reshape(step, chans, FREQ)
        return carry

    lax.fori_loop(0, nb // step, spectra, 0)

    sign = 1.0 - 2.0 * lax.bitwise_and(
        lax.broadcasted_iota(jnp.int32, (1, 1, FREQ), 2), 1
    ).astype(F32)
    chunk = 32

    def turn(re, im):
        rehi, relo = split2(re.reshape(-1, BLK))
        imhi, imlo = split2(im.reshape(-1, BLK))
        wide = jnp.concatenate([rehi, imhi, relo, imlo, rehi, imhi], axis=1)
        return mm(wide, g_ref[...]).reshape(-1, chans, BLK)

    def long(c, carry):
        p1, p2, p3 = carry
        at = c * chunk
        hre, him, hny = h_ref[0][None], h_ref[1][None], h_ref[2][None]
        window = az_ref[pl.ds(at + 1, chunk)] + sign * az_ref[pl.ds(at, chunk)]
        zre, zim = window[:, :, :BLK], window[:, :, BLK:]
        own = ad_ref[pl.ds(at, chunk)]
        ore, oim = own[:, :, :BLK], own[:, :, BLK:]
        p1 = p1 + jnp.sum(ore * zre, axis=0)
        p2 = p2 + jnp.sum(oim * zim, axis=0)
        p3 = p3 + jnp.sum(oim * zre - ore * zim, axis=0)
        both = own + sign * ad_ref[pl.ds(at + 1, chunk)]
        dre, dim = both[:, :, :BLK], both[:, :, BLK:]
        turned = turn(
            jnp.concatenate([zre * hre - zim * him, dre * hre + dim * him]),
            jnp.concatenate([zim * hny + zre * him, dim * hny - dre * him]),
        )
        y, dz = turned[:chunk], turned[chunk:]
        dm_ref[0, pl.ds(at, chunk)] = (xd_ref[pl.ds(at + 1, chunk)].astype(F32) * y).astype(BF16)
        dm_ref[1, pl.ds(at, chunk)] = (dz * v_ref[pl.ds(at, chunk)]).astype(BF16)
        dm_ref[2, pl.ds(at, chunk)] = (dz * k_ref[pl.ds(at, chunk)]).astype(BF16)
        return p1, p2, p3

    p1, p2, p3 = lax.fori_loop(0, nb // chunk, long, (zero, zero, zero))
    lre = p1 + jnp.where(lane == 0, 0.0, p2)
    lim = jnp.where(lane == 0, p2, p3)
    longs = turn(lre[None], lim[None])[0]
    graw_ref[0] = longs

    dm_ref[:, nb] = jnp.zeros((3, chans, BLK), BF16)
    out_ref[:, 0] = jnp.zeros((3, chans, BLK), BF16)
    for extra in range(nb + 1, out_ref.shape[1]):
        out_ref[:, extra] = jnp.zeros((3, chans, BLK), BF16)
    sum_ref[...] = jnp.zeros(sum_ref.shape, F32)

    def back(c, carry):
        at = c * group
        here = dm_ref[:, pl.ds(at, group)].reshape(3 * group, chans, BLK)
        after = dm_ref[:, pl.ds(at + 1, group)].reshape(3 * group, chans, BLK)
        totals = [0.0] * 3

        def tap(i, moved):
            for m in range(3):
                stream = x_refs[m][pl.ds(at + 1, group)].astype(F32)
                part = moved[m * group : (m + 1) * group]
                totals[m] += w_ref[m * STAP + i][None] * part
                sum_ref[m * STAP + i] += jnp.sum(stream * part, axis=0)

        tap(0, here.astype(F32))
        for i, moved in enumerate(moved_blocks(here, after, bs_ref), 1):
            tap(i, moved)
        for m in range(3):
            out_ref[m, pl.ds(at + 1, group)] = totals[m].astype(BF16)
        return carry

    lax.fori_loop(0, nb // group, back, 0)
    shorts = zero
    for i in range(3 * STAP):
        column = jnp.sum(sum_ref[i], axis=1, keepdims=True)
        shorts = jnp.where(lane == i, column, shorts)
    graw_ref[1] = shorts
    squares = jnp.sum(longs * longs + shorts * shorts, axis=0, keepdims=True)
    sq_ref[...] = jnp.broadcast_to(jnp.sum(squares, axis=1, keepdims=True), (1, BLK))

    def unpack(j, carry):
        offset = off_ref[j]
        kept = []
        for part in range(3):
            aligned, block, turned = place(offset, part)
            back_by = lax.bitwise_and(BLK - turned, 127)
            early = lane < turned
            for n in range(3):
                both = jnp.where(early, out_ref[part, block + n + 1], out_ref[part, block + n])
                kept.append(pltpu.roll(both, back_by, 1))
        shared = jnp.where(lane < 64, kept[2], kept[3])
        blocks = [kept[0], kept[1], shared, kept[4], kept[5], kept[6], kept[7], kept[8]]
        for n, block in enumerate(blocks):
            o_ref[j, :, n * BLK : (n + 1) * BLK] = block
        return carry

    lax.fori_loop(0, pieces, unpack, 0, unroll=2)


def solution(mesh):
    ctx = mesh.shape["ctx"]
    cores = min(2, mesh.shape["dp"])
    finer = Mesh(mesh.devices.reshape(-1, cores, 4, ctx // 4), ("z", "core", "x", "y"))
    (fh, fl), (gh, gl) = dft_tables()
    past, future = shift_tables()
    forward = np.concatenate([fh, fl])
    backward = np.concatenate([gh, gh, gl])
    smem = pl.BlockSpec(memory_space=pltpu.SMEM)
    vmem = pl.BlockSpec(memory_space=pltpu.VMEM)

    def local(streams, cotangent, counts, short_filters, long_filter):
        slots, channels = streams.shape[2:]
        own = channels // ctx
        length = 8192
        nb = length // BLK
        total_params = float((LTAP + 3 * STAP) * channels * mesh.shape["dp"])

        turned = pl.pallas_call(
            turn_out_kernel,
            out_shape=jax.ShapeDtypeStruct((channels, 4 * slots), BF16),
            in_specs=[smem, vmem, vmem],
            out_specs=vmem,
            name="turn_out",
        )(counts, streams, cotangent)
        pieces = lax.all_to_all(
            turned.reshape(ctx, own, 4 * slots), CTX, 0, 0, tiled=True
        )
        marks = pieces[:, 0, 3 * slots :].astype(F32) < 2.0**50
        live = jnp.sum(marks.astype(jnp.int32), axis=1)
        order = jnp.arange(ctx, dtype=jnp.int32)
        offsets = jnp.sum(jnp.where(order[None, :] < order[:, None], live[None, :], 0), axis=1)

        taps = long_filter.T
        spectrum = mm(jnp.concatenate([taps, taps], axis=1), jnp.asarray(forward))
        first = jnp.arange(BLK)[None, :] == 0
        hre, him = spectrum[:, :BLK], spectrum[:, BLK:]
        filters = jnp.stack([hre, jnp.where(first, 0.0, him), jnp.where(first, him, hre)])
        weights = jnp.broadcast_to(
            short_filters.reshape(3 * STAP, own, 1).astype(F32), (3 * STAP, own, BLK)
        )

        padded = nb + 4
        grads, raw, shared = pl.pallas_call(
            core_kernel,
            out_shape=(
                jax.ShapeDtypeStruct((ctx, own, 8 * BLK), BF16),
                jax.ShapeDtypeStruct((2, own, BLK), F32),
                jax.ShapeDtypeStruct((1, BLK), F32),
            ),
            in_specs=[smem] + [vmem] * 7,
            out_specs=(vmem, vmem, vmem),
            scratch_shapes=[
                pltpu.VMEM((padded, own, BLK), BF16),
                pltpu.VMEM((padded, own, BLK), BF16),
                pltpu.VMEM((padded, own, BLK), BF16),
                pltpu.VMEM((padded, own, BLK), BF16),
                pltpu.VMEM((nb, own, BLK), F32),
                pltpu.VMEM((nb, own, BLK), F32),
                pltpu.VMEM((nb, own, BLK), BF16),
                pltpu.VMEM((nb, own, BLK), BF16),
                pltpu.VMEM((nb + 1, own, FREQ), F32),
                pltpu.VMEM((nb + 1, own, FREQ), F32),
                pltpu.VMEM((3, nb + 1, own, BLK), BF16),
                pltpu.VMEM((3, padded, own, BLK), BF16),
                pltpu.VMEM((3 * STAP, own, BLK), F32),
            ],
            compiler_params=pltpu.CompilerParams(vmem_limit_bytes=40 << 20),
            name="core",
        )(
            offsets, pieces, filters, weights, jnp.asarray(forward), jnp.asarray(backward),
            jnp.asarray(past), jnp.asarray(future),
        )

        back = lax.all_to_all(grads, CTX, 0, 0, tiled=True)
        for axis in (DP, "x"):
            shared = jnp.sum(lax.all_gather(shared, axis, axis=0, tiled=True), axis=0, keepdims=True)
        shared = jnp.broadcast_to(shared, (lax.axis_size("y"), BLK))
        short_raw = raw[1, :, : 3 * STAP].T.reshape(3, STAP, own)
        shared, back, short_raw = lax.optimization_barrier((shared, back, short_raw))
        shared = lax.all_to_all(shared, "y", 0, 0, tiled=True)
        stream_grads = pl.pallas_call(
            turn_back_kernel,
            out_shape=jax.ShapeDtypeStruct((3, 1, slots, channels), BF16),
            in_specs=[smem, vmem],
            out_specs=vmem,
            name="turn_back",
        )(counts, back.reshape(channels, 8 * BLK))

        rms = jnp.sqrt(jnp.sum(shared[:, 0]) / total_params + 1e-06)
        long_grad = (raw[0] / rms).T
        short_grad = short_raw / rms
        return stream_grads, long_grad, short_grad

    return jax.shard_map(
        local,
        mesh=finer,
        in_specs=(
            P(None, None, CTX, DP),
            P(None, CTX, DP),
            P(None, CTX),
            P(None, None, DP + CTX),
            P(None, DP + CTX),
        ),
        out_specs=(
            P(None, None, CTX, DP),
            P(None, DP + CTX),
            P(None, None, DP + CTX),
        ),
        check_vma=False,
    )
```

```python
import jax
import jax.numpy as jnp
import numpy as np
from jax import lax
from jax.experimental import pallas as pl
from jax.experimental.pallas import tpu as pltpu
from jax.sharding import Mesh
from jax.sharding import PartitionSpec as P

LTAP = 128
STAP = 7
BLK = 128
FREQ = 2 * BLK
DEAD = 2.0**100
F32 = jnp.float32
BF16 = jnp.bfloat16
DP = ("z", "core")
CTX = ("x", "y")


def split_np(matrix):
    high = matrix.astype(jnp.bfloat16)
    low = (matrix - high.astype(np.float64)).astype(jnp.bfloat16)
    return high, low


def dft_tables():
    n = np.arange(BLK)[:, None]
    k = np.arange(BLK)[None, :]
    angle = 2.0 * np.pi * ((n * k) % FREQ) / FREQ
    cosines, sines = np.cos(angle), -np.sin(angle)
    nyquist = np.where(n % 2 == 0, 1.0, -1.0)
    sines[:, :1] = nyquist
    forward = np.concatenate([cosines, sines], axis=1)
    weight = np.full((FREQ, 1), 2.0 / FREQ)
    weight[0] = weight[BLK] = 1.0 / FREQ
    backward = forward.T * weight
    return split_np(forward), split_np(backward)


def shift_tables():
    row = np.arange(FREQ)[:, None]
    col = np.arange(BLK)[None, :]
    past = [row == BLK + col - i for i in range(1, STAP)]
    future = [row == col + i for i in range(1, STAP)]
    return tuple(np.concatenate(t, axis=1).astype(jnp.bfloat16) for t in (past, future))


def split2(x):
    high = x.astype(BF16)
    return high, (x - high.astype(F32)).astype(BF16)


def mm(a, b):
    return jnp.dot(a, b, preferred_element_type=F32)


def mm_nt(a, b):
    return lax.dot_general(a, b, (((1,), (1,)), ((), ())), preferred_element_type=F32)


def identity(size):
    rows = lax.broadcasted_iota(jnp.int32, (size, size), 0)
    cols = lax.broadcasted_iota(jnp.int32, (size, size), 1)
    return jnp.where(rows == cols, 1.0, 0.0).astype(BF16)


def turn_out_kernel(count_ref, s_ref, d_ref, o_ref):
    slots = s_ref.shape[2]
    channels = s_ref.shape[3]
    count = count_ref[0, 0]
    wide = min(256, channels)
    eye = identity(wide)
    lane = lax.broadcasted_iota(jnp.int32, (wide, BLK), 1)
    for first in range(0, 4 * slots, BLK):
        pieces, token, fill = [], lane, 0.0
        part, at = divmod(first, slots)
        fill = DEAD if part == 3 else 0.0
        rest = min(BLK, slots - at)
        token = lane + at
        for p, low, size in ((part, at, rest), (part + 1, 0, BLK - rest)):
            if size:
                pieces.append(s_ref[p, 0, low : low + size] if p < 3 else d_ref[0, low : low + size])
        if rest < BLK:
            token = jnp.where(lane < rest, token, lane - rest)
            fill = jnp.where(lane < rest, fill, DEAD if part == 2 else 0.0)
        rows = pieces[0] if len(pieces) == 1 else jnp.concatenate(pieces, axis=0)
        for c in range(0, channels, wide):
            kept = jnp.where(token < count, mm_nt(eye, rows[:, c : c + wide]), fill)
            o_ref[c : c + wide, first : first + BLK] = kept.astype(BF16)


def turn_back_kernel(count_ref, r_ref, o_ref):
    slots = o_ref.shape[2]
    channels = o_ref.shape[3]
    count = count_ref[0, 0]
    eye = identity(BLK)
    row = lax.broadcasted_iota(jnp.int32, (BLK, channels), 0)
    for first in range(0, 3 * slots, BLK):
        turned = mm_nt(eye, r_ref[:, first : first + BLK])
        part, at = divmod(first, slots)
        rest = min(BLK, slots - at)
        kept = jnp.where(row[:rest] + at < count, turned[:rest], 0.0).astype(BF16)
        o_ref[part, 0, at : at + rest] = kept
        if rest < BLK and part < 2:
            kept = jnp.where(row[: BLK - rest] < count, turned[rest:], 0.0).astype(BF16)
            o_ref[part + 1, 0, : BLK - rest] = kept


def core_kernel(
    off_ref, r_ref, h_ref, w_ref, f_ref, g_ref, fs_ref, bs_ref,
    o_ref, graw_ref, sq_ref,
    xq_ref, xk_ref, xv_ref, xd_ref, k_ref, v_ref, z_ref, d_ref, az_ref, ad_ref, dm_ref, out_ref, sum_ref,
):
    pieces, chans, _ = r_ref.shape
    slots = r_ref.shape[2] // 4
    nb = z_ref.shape[0]
    lane = lax.broadcasted_iota(jnp.int32, (chans, BLK), 1)

    none = jnp.zeros((chans, BLK), BF16)
    x_refs = (xq_ref, xk_ref, xv_ref, xd_ref)
    for ref in x_refs:
        ref[...] = jnp.zeros(ref.shape, BF16)

    def place(offset, part):
        aligned = part * slots // BLK * BLK
        base = offset - (part * slots - aligned)
        return aligned, lax.shift_right_arithmetic(base, 7) + 1, lax.bitwise_and(base, 127)

    def pack(j, carry):
        offset = off_ref[j]
        for part in range(4):
            aligned, block, turn = place(offset, part)
            skip = part * slots - aligned
            rolled = []
            for n in range(3):
                piece = r_ref[j, :, aligned + n * BLK : aligned + (n + 1) * BLK]
                if part == 3:
                    piece = jnp.where(piece > 2.0**50, none, piece)
                if n * BLK < skip:
                    piece = jnp.where(lane >= skip - n * BLK, piece, none)
                if (n + 1) * BLK > skip + slots:
                    piece = jnp.where(lane < skip + slots - n * BLK, piece, none)
                rolled.append(pltpu.roll(piece, turn, 1))
            early = lane < turn
            fresh = jnp.where(early, rolled[0], rolled[1])
            x_ref = x_refs[part]
            x_ref[block] += jnp.where(early, none, rolled[0])
            x_ref[block + 1] = x_ref[block + 1] + fresh if skip else fresh
            x_ref[block + 2] = jnp.where(early, rolled[1], rolled[2])
            x_ref[block + 3] = jnp.where(early, rolled[2], none)
        return carry

    lax.fori_loop(0, pieces, pack, 0, unroll=2)

    zero = jnp.zeros((chans, BLK), F32)
    group = 32

    def moved_blocks(first, second, table_ref):
        pairs = jnp.concatenate([first.reshape(-1, BLK), second.reshape(-1, BLK)], axis=1)
        for at in range(0, (STAP - 1) * BLK, FREQ):
            both = mm(pairs, table_ref[:, at : at + FREQ])
            yield both[:, :BLK].reshape(-1, chans, BLK)
            yield both[:, BLK:].reshape(-1, chans, BLK)

    def features(c, carry):
        at = c * group
        before = jnp.concatenate([x_refs[m][pl.ds(at, group)] for m in range(3)])
        here = jnp.concatenate([x_refs[m][pl.ds(at + 1, group)] for m in range(3)])
        feats = [
            w_ref[m * STAP][None] * here[m * group : (m + 1) * group].astype(F32) for m in range(3)
        ]
        for i, moved in enumerate(moved_blocks(before, here, fs_ref), 1):
            for m in range(3):
                feats[m] += w_ref[m * STAP + i][None] * moved[m * group : (m + 1) * group]
        k_ref[pl.ds(at, group)] = feats[1]
        v_ref[pl.ds(at, group)] = feats[2]
        z_ref[pl.ds(at, group)] = (feats[1] * feats[2]).astype(BF16)
        d_ref[pl.ds(at, group)] = (xd_ref[pl.ds(at + 1, group)].astype(F32) * feats[0]).astype(BF16)
        return carry

    lax.fori_loop(0, nb // group, features, 0)

    step = 32
    az_ref[0] = jnp.zeros((chans, FREQ), F32)
    ad_ref[nb] = jnp.zeros((chans, FREQ), F32)

    def spectra(c, carry):
        at = c * step
        zs = z_ref[pl.ds(at, step)].reshape(step * chans, BLK)
        ds = d_ref[pl.ds(at, step)].reshape(step * chans, BLK)
        table = f_ref[...]
        for source, to, first in ((zs, az_ref, at + 1), (ds, ad_ref, at)):
            result = mm(jnp.concatenate([source, source], axis=1), table)
            to[pl.ds(first, step)] = result.reshape(step, chans, FREQ)
        return carry

    lax.fori_loop(0, nb // step, spectra, 0)

    sign = 1.0 - 2.0 * lax.bitwise_and(
        lax.broadcasted_iota(jnp.int32, (1, 1, FREQ), 2), 1
    ).astype(F32)
    chunk = 32

    def turn(re, im):
        rehi, relo = split2(re.reshape(-1, BLK))
        imhi, imlo = split2(im.reshape(-1, BLK))
        wide = jnp.concatenate([rehi, imhi, relo, imlo, rehi, imhi], axis=1)
        return mm(wide, g_ref[...]).reshape(-1, chans, BLK)

    def long(c, carry):
        p1, p2, p3 = carry
        at = c * chunk
        hre, him, hny = h_ref[0][None], h_ref[1][None], h_ref[2][None]
        window = az_ref[pl.ds(at + 1, chunk)] + sign * az_ref[pl.ds(at, chunk)]
        zre, zim = window[:, :, :BLK], window[:, :, BLK:]
        own = ad_ref[pl.ds(at, chunk)]
        ore, oim = own[:, :, :BLK], own[:, :, BLK:]
        p1 = p1 + jnp.sum(ore * zre, axis=0)
        p2 = p2 + jnp.sum(oim * zim, axis=0)
        p3 = p3 + jnp.sum(oim * zre - ore * zim, axis=0)
        both = own + sign * ad_ref[pl.ds(at + 1, chunk)]
        dre, dim = both[:, :, :BLK], both[:, :, BLK:]
        turned = turn(
            jnp.concatenate([zre * hre - zim * him, dre * hre + dim * him]),
            jnp.concatenate([zim * hny + zre * him, dim * hny - dre * him]),
        )
        y, dz = turned[:chunk], turned[chunk:]
        dm_ref[0, pl.ds(at, chunk)] = (xd_ref[pl.ds(at + 1, chunk)].astype(F32) * y).astype(BF16)
        dm_ref[1, pl.ds(at, chunk)] = (dz * v_ref[pl.ds(at, chunk)]).astype(BF16)
        dm_ref[2, pl.ds(at, chunk)] = (dz * k_ref[pl.ds(at, chunk)]).astype(BF16)
        return p1, p2, p3

    p1, p2, p3 = lax.fori_loop(0, nb // chunk, long, (zero, zero, zero))
    lre = p1 + jnp.where(lane == 0, 0.0, p2)
    lim = jnp.where(lane == 0, p2, p3)
    longs = turn(lre[None], lim[None])[0]
    graw_ref[0] = longs

    dm_ref[:, nb] = jnp.zeros((3, chans, BLK), BF16)
    out_ref[:, 0] = jnp.zeros((3, chans, BLK), BF16)
    for extra in range(nb + 1, out_ref.shape[1]):
        out_ref[:, extra] = jnp.zeros((3, chans, BLK), BF16)
    sum_ref[...] = jnp.zeros(sum_ref.shape, F32)

    def back(c, carry):
        at = c * group
        here = dm_ref[:, pl.ds(at, group)].reshape(3 * group, chans, BLK)
        after = dm_ref[:, pl.ds(at + 1, group)].reshape(3 * group, chans, BLK)
        totals = [0.0] * 3

        def tap(i, moved):
            for m in range(3):
                stream = x_refs[m][pl.ds(at + 1, group)].astype(F32)
                part = moved[m * group : (m + 1) * group]
                totals[m] += w_ref[m * STAP + i][None] * part
                sum_ref[m * STAP + i] += jnp.sum(stream * part, axis=0)

        tap(0, here.astype(F32))
        for i, moved in enumerate(moved_blocks(here, after, bs_ref), 1):
            tap(i, moved)
        for m in range(3):
            out_ref[m, pl.ds(at + 1, group)] = totals[m].astype(BF16)
        return carry

    lax.fori_loop(0, nb // group, back, 0)
    shorts = zero
    for i in range(3 * STAP):
        column = jnp.sum(sum_ref[i], axis=1, keepdims=True)
        shorts = jnp.where(lane == i, column, shorts)
    graw_ref[1] = shorts
    squares = jnp.sum(longs * longs + shorts * shorts, axis=0, keepdims=True)
    sq_ref[...] = jnp.broadcast_to(jnp.sum(squares, axis=1, keepdims=True), (1, BLK))

    def unpack(j, carry):
        offset = off_ref[j]
        kept = []
        for part in range(3):
            aligned, block, turned = place(offset, part)
            back_by = lax.bitwise_and(BLK - turned, 127)
            early = lane < turned
            for n in range(3):
                both = jnp.where(early, out_ref[part, block + n + 1], out_ref[part, block + n])
                kept.append(pltpu.roll(both, back_by, 1))
        shared = jnp.where(lane < 64, kept[2], kept[3])
        blocks = [kept[0], kept[1], shared, kept[4], kept[5], kept[6], kept[7], kept[8]]
        for n, block in enumerate(blocks):
            o_ref[j, :, n * BLK : (n + 1) * BLK] = block
        return carry

    lax.fori_loop(0, pieces, unpack, 0, unroll=2)


def solution(mesh):
    ctx = mesh.shape["ctx"]
    cores = min(2, mesh.shape["dp"])
    finer = Mesh(mesh.devices.reshape(-1, cores, 4, ctx // 4), ("z", "core", "x", "y"))
    (fh, fl), (gh, gl) = dft_tables()
    past, future = shift_tables()
    forward = np.concatenate([fh, fl])
    backward = np.concatenate([gh, gh, gl])
    smem = pl.BlockSpec(memory_space=pltpu.SMEM)
    vmem = pl.BlockSpec(memory_space=pltpu.VMEM)

    def local(streams, cotangent, counts, short_filters, long_filter):
        slots, channels = streams.shape[2:]
        own = channels // ctx
        share = 256
        length = 8192
        nb = length // BLK
        total_params = float((LTAP + 3 * STAP) * channels * mesh.shape["dp"])

        turned = pl.pallas_call(
            turn_out_kernel,
            out_shape=jax.ShapeDtypeStruct((channels, 4 * slots), BF16),
            grid=(channels // share,),
            in_specs=[
                smem,
                pl.BlockSpec((3, 1, slots, share), lambda c: (0, 0, 0, c)),
                pl.BlockSpec((1, slots, share), lambda c: (0, 0, c)),
            ],
            out_specs=pl.BlockSpec((share, 4 * slots), lambda c: (c, 0)),
            name="turn_out",
        )(counts, streams, cotangent)
        pieces = lax.all_to_all(
            turned.reshape(ctx, own, 4 * slots), CTX, 0, 0, tiled=True
        )
        marks = pieces[:, 0, 3 * slots :].astype(F32) < 2.0**50
        live = jnp.sum(marks.astype(jnp.int32), axis=1)
        order = jnp.arange(ctx, dtype=jnp.int32)
        offsets = jnp.sum(jnp.where(order[None, :] < order[:, None], live[None, :], 0), axis=1)

        taps = long_filter.T
        spectrum = mm(jnp.concatenate([taps, taps], axis=1), jnp.asarray(forward))
        first = jnp.arange(BLK)[None, :] == 0
        hre, him = spectrum[:, :BLK], spectrum[:, BLK:]
        filters = jnp.stack([hre, jnp.where(first, 0.0, him), jnp.where(first, him, hre)])
        weights = jnp.broadcast_to(
            short_filters.reshape(3 * STAP, own, 1).astype(F32), (3 * STAP, own, BLK)
        )

        padded = nb + 4
        grads, raw, shared = pl.pallas_call(
            core_kernel,
            out_shape=(
                jax.ShapeDtypeStruct((ctx, own, 8 * BLK), BF16),
                jax.ShapeDtypeStruct((2, own, BLK), F32),
                jax.ShapeDtypeStruct((1, BLK), F32),
            ),
            in_specs=[smem] + [vmem] * 7,
            out_specs=(vmem, vmem, vmem),
            scratch_shapes=[
                pltpu.VMEM((padded, own, BLK), BF16),
                pltpu.VMEM((padded, own, BLK), BF16),
                pltpu.VMEM((padded, own, BLK), BF16),
                pltpu.VMEM((padded, own, BLK), BF16),
                pltpu.VMEM((nb, own, BLK), F32),
                pltpu.VMEM((nb, own, BLK), F32),
                pltpu.VMEM((nb, own, BLK), BF16),
                pltpu.VMEM((nb, own, BLK), BF16),
                pltpu.VMEM((nb + 1, own, FREQ), F32),
                pltpu.VMEM((nb + 1, own, FREQ), F32),
                pltpu.VMEM((3, nb + 1, own, BLK), BF16),
                pltpu.VMEM((3, padded, own, BLK), BF16),
                pltpu.VMEM((3 * STAP, own, BLK), F32),
            ],
            compiler_params=pltpu.CompilerParams(vmem_limit_bytes=40 << 20),
            name="core",
        )(
            offsets, pieces, filters, weights, jnp.asarray(forward), jnp.asarray(backward),
            jnp.asarray(past), jnp.asarray(future),
        )

        back = lax.all_to_all(grads, CTX, 0, 0, tiled=True)
        for axis in (DP, "x"):
            shared = jnp.sum(lax.all_gather(shared, axis, axis=0, tiled=True), axis=0, keepdims=True)
        shared = jnp.broadcast_to(shared, (lax.axis_size("y"), BLK))
        short_raw = raw[1, :, : 3 * STAP].T.reshape(3, STAP, own)
        shared, back, short_raw = lax.optimization_barrier((shared, back, short_raw))
        shared = lax.all_to_all(shared, "y", 0, 0, tiled=True)
        stream_grads = pl.pallas_call(
            turn_back_kernel,
            out_shape=jax.ShapeDtypeStruct((3, 1, slots, channels), BF16),
            grid=(channels // share,),
            in_specs=[smem, pl.BlockSpec((share, 8 * BLK), lambda c: (c, 0))],
            out_specs=pl.BlockSpec((3, 1, slots, share), lambda c: (0, 0, 0, c)),
            name="turn_back",
        )(counts, back.reshape(channels, 8 * BLK))

        rms = jnp.sqrt(jnp.sum(shared, axis=0) / total_params + 1e-06)
        long_grad = (raw[0] / rms[None]).T
        short_grad = short_raw / rms[:own]
        return stream_grads, long_grad, short_grad

    return jax.shard_map(
        local,
        mesh=finer,
        in_specs=(
            P(None, None, CTX, DP),
            P(None, CTX, DP),
            P(None, CTX),
            P(None, None, DP + CTX),
            P(None, DP + CTX),
        ),
        out_specs=(
            P(None, None, CTX, DP),
            P(None, DP + CTX),
            P(None, None, DP + CTX),
        ),
        check_vma=False,
    )
```

```python
import jax
import jax.numpy as jnp
import numpy as np
from jax import lax
from jax.experimental import pallas as pl
from jax.experimental.pallas import tpu as pltpu
from jax.sharding import Mesh
from jax.sharding import PartitionSpec as P


LTAP = 128
STAP = 7
BLK = 128
FREQ = 2 * BLK
DEAD = 2.0**100
F32 = jnp.float32
BF16 = jnp.bfloat16
DP = ("z", "core")
CTX = ("x", "y")


def split_np(matrix):
    high = matrix.astype(jnp.bfloat16)
    low = (matrix - high.astype(np.float64)).astype(jnp.bfloat16)
    return high, low


def dft_tables():
    n = np.arange(BLK)[:, None]
    k = np.arange(BLK)[None, :]
    angle = 2.0 * np.pi * ((n * k) % FREQ) / FREQ
    cosines, sines = np.cos(angle), -np.sin(angle)
    nyquist = np.where(n % 2 == 0, 1.0, -1.0)
    sines[:, :1] = nyquist
    forward = np.concatenate([cosines, sines], axis=1)
    weight = np.full((FREQ, 1), 2.0 / FREQ)
    weight[0] = weight[BLK] = 1.0 / FREQ
    backward = forward.T * weight
    return split_np(forward), split_np(backward)


def shift_tables():
    row = np.arange(FREQ)[:, None]
    col = np.arange(BLK)[None, :]
    past = [row == BLK + col - i for i in range(1, STAP)]
    future = [row == col + i for i in range(1, STAP)]
    return tuple(np.concatenate(t, axis=1).astype(jnp.bfloat16) for t in (past, future))


def split2(x):
    high = x.astype(BF16)
    return high, (x - high.astype(F32)).astype(BF16)


def mm(a, b):
    return jnp.dot(a, b, preferred_element_type=F32)


def mm_nt(a, b):
    return lax.dot_general(a, b, (((1,), (1,)), ((), ())), preferred_element_type=F32)


def identity(size):
    rows = lax.broadcasted_iota(jnp.int32, (size, size), 0)
    cols = lax.broadcasted_iota(jnp.int32, (size, size), 1)
    return jnp.where(rows == cols, 1.0, 0.0).astype(BF16)


def turn_out_kernel(count_ref, s_ref, d_ref, o_ref):
    slots = s_ref.shape[2]
    channels = s_ref.shape[3]
    count = count_ref[0, 0]
    wide = min(256, channels)
    eye = identity(wide)
    lane = lax.broadcasted_iota(jnp.int32, (wide, BLK), 1)
    for first in range(0, 4 * slots, BLK):
        pieces, token, fill = [], lane, 0.0
        part, at = divmod(first, slots)
        fill = DEAD if part == 3 else 0.0
        rest = min(BLK, slots - at)
        token = lane + at
        for p, low, size in ((part, at, rest), (part + 1, 0, BLK - rest)):
            if size:
                pieces.append(s_ref[p, 0, low : low + size] if p < 3 else d_ref[0, low : low + size])
        if rest < BLK:
            token = jnp.where(lane < rest, token, lane - rest)
            fill = jnp.where(lane < rest, fill, DEAD if part == 2 else 0.0)
        rows = pieces[0] if len(pieces) == 1 else jnp.concatenate(pieces, axis=0)
        for c in range(0, channels, wide):
            kept = jnp.where(token < count, mm_nt(eye, rows[:, c : c + wide]), fill)
            o_ref[c : c + wide, first : first + BLK] = kept.astype(BF16)


def turn_back_kernel(count_ref, r_ref, o_ref):
    slots = o_ref.shape[2]
    channels = o_ref.shape[3]
    count = count_ref[0, 0]
    eye = identity(BLK)
    row = lax.broadcasted_iota(jnp.int32, (BLK, channels), 0)
    for first in range(0, 3 * slots, BLK):
        turned = mm_nt(eye, r_ref[:, first : first + BLK])
        part, at = divmod(first, slots)
        rest = min(BLK, slots - at)
        kept = jnp.where(row[:rest] + at < count, turned[:rest], 0.0).astype(BF16)
        o_ref[part, 0, at : at + rest] = kept
        if rest < BLK and part < 2:
            kept = jnp.where(row[: BLK - rest] < count, turned[rest:], 0.0).astype(BF16)
            o_ref[part + 1, 0, : BLK - rest] = kept


def core_kernel(
    off_ref, r_ref, h_ref, w_ref, f_ref, g_ref, fs_ref, bs_ref,
    o_ref, graw_ref, sq_ref,
    xq_ref, xk_ref, xv_ref, xd_ref, k_ref, v_ref, z_ref, d_ref, az_ref, ad_ref, dm_ref, out_ref, sum_ref,
):
    pieces, chans, _ = r_ref.shape
    slots = r_ref.shape[2] // 4
    nb = z_ref.shape[0]
    lane = lax.broadcasted_iota(jnp.int32, (chans, BLK), 1)

    none = jnp.zeros((chans, BLK), BF16)
    x_refs = (xq_ref, xk_ref, xv_ref, xd_ref)
    for ref in x_refs:
        ref[...] = jnp.zeros(ref.shape, BF16)

    def place(offset, part):
        aligned = part * slots // BLK * BLK
        base = offset - (part * slots - aligned)
        return aligned, lax.shift_right_arithmetic(base, 7) + 1, lax.bitwise_and(base, 127)

    def pack(j, carry):
        offset = off_ref[j]
        for part in range(4):
            aligned, block, turn = place(offset, part)
            skip = part * slots - aligned
            rolled = []
            for n in range(3):
                piece = r_ref[j, :, aligned + n * BLK : aligned + (n + 1) * BLK]
                if part == 3:
                    piece = jnp.where(piece > 2.0**50, none, piece)
                if n * BLK < skip:
                    piece = jnp.where(lane >= skip - n * BLK, piece, none)
                if (n + 1) * BLK > skip + slots:
                    piece = jnp.where(lane < skip + slots - n * BLK, piece, none)
                rolled.append(pltpu.roll(piece, turn, 1))
            early = lane < turn
            fresh = jnp.where(early, rolled[0], rolled[1])
            x_ref = x_refs[part]
            x_ref[block] += jnp.where(early, none, rolled[0])
            x_ref[block + 1] = x_ref[block + 1] + fresh if skip else fresh
            x_ref[block + 2] = jnp.where(early, rolled[1], rolled[2])
            x_ref[block + 3] = jnp.where(early, rolled[2], none)
        return carry

    lax.fori_loop(0, pieces, pack, 0, unroll=2)

    zero = jnp.zeros((chans, BLK), F32)
    group = 64

    def moved_blocks(first, second, table_ref):
        pairs = jnp.concatenate([first.reshape(-1, BLK), second.reshape(-1, BLK)], axis=1)
        for at in range(0, (STAP - 1) * BLK, FREQ):
            both = mm(pairs, table_ref[:, at : at + FREQ])
            yield both[:, :BLK].reshape(-1, chans, BLK)
            yield both[:, BLK:].reshape(-1, chans, BLK)

    def features(c, carry):
        at = c * group
        before = jnp.concatenate([x_refs[m][pl.ds(at, group)] for m in range(3)])
        here = jnp.concatenate([x_refs[m][pl.ds(at + 1, group)] for m in range(3)])
        feats = [
            w_ref[m * STAP][None] * here[m * group : (m + 1) * group].astype(F32) for m in range(3)
        ]
        for i, moved in enumerate(moved_blocks(before, here, fs_ref), 1):
            for m in range(3):
                feats[m] += w_ref[m * STAP + i][None] * moved[m * group : (m + 1) * group]
        k_ref[pl.ds(at, group)] = feats[1]
        v_ref[pl.ds(at, group)] = feats[2]
        z_ref[pl.ds(at, group)] = (feats[1] * feats[2]).astype(BF16)
        d_ref[pl.ds(at, group)] = (xd_ref[pl.ds(at + 1, group)].astype(F32) * feats[0]).astype(BF16)
        return carry

    lax.fori_loop(0, nb // group, features, 0)

    step = 32
    az_ref[0] = jnp.zeros((chans, FREQ), F32)
    ad_ref[nb] = jnp.zeros((chans, FREQ), F32)

    def spectra(c, carry):
        at = c * step
        zs = z_ref[pl.ds(at, step)].reshape(step * chans, BLK)
        ds = d_ref[pl.ds(at, step)].reshape(step * chans, BLK)
        table = f_ref[...]
        for source, to, first in ((zs, az_ref, at + 1), (ds, ad_ref, at)):
            result = mm(jnp.concatenate([source, source], axis=1), table)
            to[pl.ds(first, step)] = result.reshape(step, chans, FREQ)
        return carry

    lax.fori_loop(0, nb // step, spectra, 0)

    sign = 1.0 - 2.0 * lax.bitwise_and(
        lax.broadcasted_iota(jnp.int32, (1, 1, FREQ), 2), 1
    ).astype(F32)
    chunk = 64

    def turn(re, im):
        rehi, relo = split2(re.reshape(-1, BLK))
        imhi, imlo = split2(im.reshape(-1, BLK))
        wide = jnp.concatenate([rehi, imhi, relo, imlo, rehi, imhi], axis=1)
        return mm(wide, g_ref[...]).reshape(-1, chans, BLK)

    def long(c, carry):
        p1, p2, p3 = carry
        at = c * chunk
        hre, him, hny = h_ref[0][None], h_ref[1][None], h_ref[2][None]
        window = az_ref[pl.ds(at + 1, chunk)] + sign * az_ref[pl.ds(at, chunk)]
        zre, zim = window[:, :, :BLK], window[:, :, BLK:]
        own = ad_ref[pl.ds(at, chunk)]
        ore, oim = own[:, :, :BLK], own[:, :, BLK:]
        p1 = p1 + jnp.sum(ore * zre, axis=0)
        p2 = p2 + jnp.sum(oim * zim, axis=0)
        p3 = p3 + jnp.sum(oim * zre - ore * zim, axis=0)
        both = own + sign * ad_ref[pl.ds(at + 1, chunk)]
        dre, dim = both[:, :, :BLK], both[:, :, BLK:]
        turned = turn(
            jnp.concatenate([zre * hre - zim * him, dre * hre + dim * him]),
            jnp.concatenate([zim * hny + zre * him, dim * hny - dre * him]),
        )
        y, dz = turned[:chunk], turned[chunk:]
        dm_ref[0, pl.ds(at, chunk)] = (xd_ref[pl.ds(at + 1, chunk)].astype(F32) * y).astype(BF16)
        dm_ref[1, pl.ds(at, chunk)] = (dz * v_ref[pl.ds(at, chunk)]).astype(BF16)
        dm_ref[2, pl.ds(at, chunk)] = (dz * k_ref[pl.ds(at, chunk)]).astype(BF16)
        return p1, p2, p3

    p1, p2, p3 = lax.fori_loop(0, nb // chunk, long, (zero, zero, zero))
    lre = p1 + jnp.where(lane == 0, 0.0, p2)
    lim = jnp.where(lane == 0, p2, p3)
    longs = turn(lre[None], lim[None])[0]
    graw_ref[0] = longs

    dm_ref[:, nb] = jnp.zeros((3, chans, BLK), BF16)
    out_ref[:, 0] = jnp.zeros((3, chans, BLK), BF16)
    for extra in range(nb + 1, out_ref.shape[1]):
        out_ref[:, extra] = jnp.zeros((3, chans, BLK), BF16)
    sum_ref[...] = jnp.zeros(sum_ref.shape, F32)

    def back(c, carry):
        at = c * group
        here = dm_ref[:, pl.ds(at, group)].reshape(3 * group, chans, BLK)
        after = dm_ref[:, pl.ds(at + 1, group)].reshape(3 * group, chans, BLK)
        totals = [0.0] * 3

        def tap(i, moved):
            for m in range(3):
                stream = x_refs[m][pl.ds(at + 1, group)].astype(F32)
                part = moved[m * group : (m + 1) * group]
                totals[m] += w_ref[m * STAP + i][None] * part
                sum_ref[m * STAP + i] += jnp.sum(stream * part, axis=0)

        tap(0, here.astype(F32))
        for i, moved in enumerate(moved_blocks(here, after, bs_ref), 1):
            tap(i, moved)
        for m in range(3):
            out_ref[m, pl.ds(at + 1, group)] = totals[m].astype(BF16)
        return carry

    lax.fori_loop(0, nb // group, back, 0)
    shorts = zero
    for i in range(3 * STAP):
        column = jnp.sum(sum_ref[i], axis=1, keepdims=True)
        shorts = jnp.where(lane == i, column, shorts)
    graw_ref[1] = shorts
    squares = jnp.sum(longs * longs + shorts * shorts, axis=0, keepdims=True)
    sq_ref[...] = jnp.broadcast_to(jnp.sum(squares, axis=1, keepdims=True), (1, BLK))

    def unpack(j, carry):
        offset = off_ref[j]
        kept = []
        for part in range(3):
            _, block, turned = place(offset, part)
            back_by = lax.bitwise_and(BLK - turned, 127)
            early = lane < turned
            for n in range(3):
                both = jnp.where(early, out_ref[part, block + n + 1], out_ref[part, block + n])
                kept.append(pltpu.roll(both, back_by, 1))
        shared = jnp.where(lane < 64, kept[2], kept[3])
        blocks = [kept[0], kept[1], shared, kept[4], kept[5], kept[6], kept[7], kept[8]]
        for n, block in enumerate(blocks):
            o_ref[j, :, n * BLK : (n + 1) * BLK] = block
        return carry

    lax.fori_loop(0, pieces, unpack, 0, unroll=2)


def solution(mesh):
    ctx = mesh.shape["ctx"]
    cores = min(2, mesh.shape["dp"])
    finer = Mesh(mesh.devices.reshape(-1, cores, 4, ctx // 4), ("z", "core", "x", "y"))
    (fh, fl), (gh, gl) = dft_tables()
    past, future = shift_tables()
    forward = np.concatenate([fh, fl])
    backward = np.concatenate([gh, gh, gl])
    smem = pl.BlockSpec(memory_space=pltpu.SMEM)
    vmem = pl.BlockSpec(memory_space=pltpu.VMEM)

    def local(streams, cotangent, counts, short_filters, long_filter):
        slots, channels = streams.shape[2:]
        own = channels // ctx
        share = 256
        length = 8192
        nb = length // BLK
        total_params = float((LTAP + 3 * STAP) * channels * mesh.shape["dp"])

        turned = pl.pallas_call(
            turn_out_kernel,
            out_shape=jax.ShapeDtypeStruct((channels, 4 * slots), BF16),
            grid=(channels // share,),
            in_specs=[
                smem,
                pl.BlockSpec((3, 1, slots, share), lambda c: (0, 0, 0, c)),
                pl.BlockSpec((1, slots, share), lambda c: (0, 0, c)),
            ],
            out_specs=pl.BlockSpec((share, 4 * slots), lambda c: (c, 0)),
            name="turn_out",
        )(counts, streams, cotangent)
        pieces = lax.all_to_all(
            turned.reshape(ctx, own, 4 * slots), CTX, 0, 0, tiled=True
        )
        marks = pieces[:, 0, 3 * slots :].astype(F32) < 2.0**50
        live = jnp.sum(marks.astype(jnp.int32), axis=1)
        order = jnp.arange(ctx, dtype=jnp.int32)
        offsets = jnp.sum(jnp.where(order[None, :] < order[:, None], live[None, :], 0), axis=1)

        taps = long_filter.T
        spectrum = mm(jnp.concatenate([taps, taps], axis=1), jnp.asarray(forward))
        first = jnp.arange(BLK)[None, :] == 0
        hre, him = spectrum[:, :BLK], spectrum[:, BLK:]
        filters = jnp.stack([hre, jnp.where(first, 0.0, him), jnp.where(first, him, hre)])
        weights = jnp.broadcast_to(
            short_filters.reshape(3 * STAP, own, 1).astype(F32), (3 * STAP, own, BLK)
        )

        padded = nb + 4
        grads, raw, shared = pl.pallas_call(
            core_kernel,
            out_shape=(
                jax.ShapeDtypeStruct((ctx, own, 8 * BLK), BF16),
                jax.ShapeDtypeStruct((2, own, BLK), F32),
                jax.ShapeDtypeStruct((1, BLK), F32),
            ),
            in_specs=[smem] + [vmem] * 7,
            out_specs=(vmem, vmem, vmem),
            scratch_shapes=[
                pltpu.VMEM((padded, own, BLK), BF16),
                pltpu.VMEM((padded, own, BLK), BF16),
                pltpu.VMEM((padded, own, BLK), BF16),
                pltpu.VMEM((padded, own, BLK), BF16),
                pltpu.VMEM((nb, own, BLK), F32),
                pltpu.VMEM((nb, own, BLK), F32),
                pltpu.VMEM((nb, own, BLK), BF16),
                pltpu.VMEM((nb, own, BLK), BF16),
                pltpu.VMEM((nb + 1, own, FREQ), F32),
                pltpu.VMEM((nb + 1, own, FREQ), F32),
                pltpu.VMEM((3, nb + 1, own, BLK), BF16),
                pltpu.VMEM((3, padded, own, BLK), BF16),
                pltpu.VMEM((3 * STAP, own, BLK), F32),
            ],
            compiler_params=pltpu.CompilerParams(vmem_limit_bytes=40 << 20),
            name="core",
        )(
            offsets, pieces, filters, weights, jnp.asarray(forward), jnp.asarray(backward),
            jnp.asarray(past), jnp.asarray(future),
        )

        back = lax.all_to_all(grads, CTX, 0, 0, tiled=True)
        for axis in (DP, "x"):
            shared = jnp.sum(lax.all_gather(shared, axis, axis=0, tiled=True), axis=0, keepdims=True)
        shared = jnp.broadcast_to(shared, (lax.axis_size("y"), BLK))
        short_raw = raw[1, :, : 3 * STAP].T.reshape(3, STAP, own)
        shared, back, short_raw = lax.optimization_barrier((shared, back, short_raw))
        shared = lax.all_to_all(shared, "y", 0, 0, tiled=True)
        stream_grads = pl.pallas_call(
            turn_back_kernel,
            out_shape=jax.ShapeDtypeStruct((3, 1, slots, channels), BF16),
            grid=(channels // share,),
            in_specs=[smem, pl.BlockSpec((share, 8 * BLK), lambda c: (c, 0))],
            out_specs=pl.BlockSpec((3, 1, slots, share), lambda c: (0, 0, 0, c)),
            name="turn_back",
        )(counts, back.reshape(channels, 8 * BLK))

        rms = jnp.sqrt(jnp.sum(shared, axis=0) / total_params + 1e-06)
        long_grad = (raw[0] / rms[None]).T
        short_grad = short_raw / rms[:own]
        return stream_grads, long_grad, short_grad

    return jax.shard_map(
        local,
        mesh=finer,
        in_specs=(
            P(None, None, CTX, DP),
            P(None, CTX, DP),
            P(None, CTX),
            P(None, None, DP + CTX),
            P(None, DP + CTX),
        ),
        out_specs=(
            P(None, None, CTX, DP),
            P(None, DP + CTX),
            P(None, None, DP + CTX),
        ),
        check_vma=False,
    )
```
